512 devices in a mesh: seg: 16 (over x, y_hi), pen: 32 (over y_lo, z, core).
Axes of the slice: x: 4, y: 8 (y_hi: 4, y_lo: 2; y = y_hi * 2 + y_lo), z: 8, core: 2. Of those that a mesh axis runs over, the one named last changes fastest.
Arguments:
- state: float32 [64, 384, 384], P('seg', 'pen'), may hold values from -6 to 6
- krylov: float32 [16, 64, 384, 384], P(None, 'seg', 'pen'), may hold values from -15 to 15
Outputs:
- residual: float32 [64, 384, 384], P('seg', 'pen')
- next_vector: float32 [64, 384, 384], P('seg', 'pen')
- hessenberg: float32 [17], replicated
The draws below stay inside these ranges and needn't reach their ends.
All inputs are finite; a program needn't handle non-finite values.
Results may differ from the reference program's by a relative error of at most 0.0003.
Values sent between devices are 32-bit elements; how exact they have to be, the bound alone decides.
No kernel may reach another device: no remote copies, remote signals or barrier semaphores. Data moves between devices by JAX's collectives and lax.ppermute only.
A program may use at most 64 MiB of HBM per device.

```python
import math
import jax
import jax.numpy as jnp
from jax import lax

NX = 384
NZ = 384
PLANES = 4
STEPS = 2
KRY = 16
SEGMENTS = 16
ROWS = 64


def draw_state(key, part):
    first_key = jax.random.fold_in(key, 0)
    return jax.random.truncated_normal(first_key, -6.0, 6.0, (ROWS, NZ, NX), jnp.float32)


def draw_krylov(key, part):
    first_key, second_key = jax.random.split(jax.random.fold_in(key, 17))
    values = jax.random.truncated_normal(first_key, -4.0, 4.0, (KRY, ROWS, NZ, NX), jnp.float32)
    mixing = jax.random.uniform(second_key, (KRY,), jnp.float32, 0.05, 0.25)
    mixing = jnp.where(jnp.arange(KRY) == KRY - 1, 0.0, mixing)
    segment = (jnp.arange(ROWS) // PLANES).astype(jnp.float32)
    rise_seg = jnp.sqrt(1.0 + 2.0 * segment / max(SEGMENTS - 1, 1))
    rise_z = jnp.sqrt(1.0 + 2.0 * jnp.arange(NZ).astype(jnp.float32) / (NZ - 1))
    mixed = values + mixing[:, None, None, None] * values[KRY - 1][None]
    return mixed * rise_seg[None, :, None, None] * rise_z[None, None, :, None]


def setup_inputs(seed: int = 0) -> dict:
    key_of = jax.random.split(jax.random.key(seed), 3)
    return {
        "state": draw_state(jax.random.fold_in(key_of[2], 71), 0),
        "krylov": draw_krylov(jax.random.fold_in(key_of[2], 71), 0),
    }


time_step = 0.0003
viscosity = 0.0226

def product(formula, former, latter):
    return jnp.einsum(formula, former, latter, precision=lax.Precision.HIGHEST, preferred_element_type=jnp.float32)

def tables(count):
    indices = jnp.arange(count, dtype=jnp.int32)
    phases = indices[:, None] * indices[None, :] % count
    angles = phases.astype(jnp.float32) * (2.0 * math.pi / count)
    cosines = jnp.cos(angles)
    sines = jnp.sin(angles)
    signed = jnp.where(indices <= count // 2, indices, indices - count).astype(jnp.float32)
    slopes = jnp.where(indices == count // 2, 0.0, signed)
    return (cosines + sines, slopes[:, None] * (cosines - sines), signed)

def tendency(z_slope, z_plain):
    stream_z = z_slope[0:2]
    vortex_z = z_slope[2:4]
    stream_x = z_plain[0:2]
    vortex_x = z_plain[2:4]
    base_term = stream_x[0] * vortex_z[0] - stream_z[0] * vortex_x[0]
    tangent_term = stream_x[1] * vortex_z[0] + stream_x[0] * vortex_z[1] - stream_z[1] * vortex_x[0] - stream_z[0] * vortex_x[1]
    return jnp.stack([base_term, tangent_term])

def reference(state, krylov):
    basis_x, slopes_x, signed_x = tables(NX)
    basis_z, slopes_z, signed_z = tables(NZ)
    ksquare = signed_z[:, None] ** 2 + signed_x[None, :] ** 2
    inverse_k = jnp.where(ksquare > 0, 1.0 / jnp.where(ksquare > 0, ksquare, 1.0), 0.0)
    damping = 1.0 / (1.0 + time_step * viscosity * ksquare)
    forward_x = basis_x / NX
    forward_z = basis_z / NZ
    direction = krylov[KRY - 1]
    fields = jnp.stack([state, direction])
    for repeat in range(STEPS):
        spectra = jnp.concatenate([fields * inverse_k, fields], 0)
        values_x = product('arzx,xj->arzj', spectra, basis_x)
        slopes_along = product('arzx,xj->arzj', spectra, slopes_x)
        z_slope = product('arzx,zj->arjx', values_x, slopes_z)
        z_plain = product('arzx,zj->arjx', slopes_along, basis_z)
        modes_z = product('arzx,zk->arkx', tendency(z_slope, z_plain), forward_z)
        forcing = product('arzx,xk->arzk', modes_z, forward_x)
        fields = (fields + time_step * forcing) * damping
    moved = jnp.roll(fields, PLANES, axis=1)
    residual = moved[0] - state
    image = moved[1] - direction
    total = float(ROWS * NZ * NX)
    coeffs = product('krzx,rzx->k', krylov, image) / total
    remain = image - product('k,krzx->rzx', coeffs, krylov)
    norm_value = jnp.sqrt(jnp.sum(remain * remain) / total + 1e-06)
    return (residual, remain / norm_value, jnp.concatenate([coeffs, norm_value[None]]))
```

```python
import functools

import jax
import jax.numpy as jnp
import numpy as np
from jax import lax
from jax.experimental import pallas as pl
from jax.experimental.pallas import tpu as pltpu
from jax.sharding import PartitionSpec as P

NX = 384
NZ = 384
PLANES = 4
STEPS = 2
KRY = 16
SEGS = 16
PEN = 32
CUT = NZ // PEN
TEAM = 8
WIDE = NZ // TEAM
TILE = 128
INTERPRET = False

time_step = 0.0003
viscosity = 0.0226


def pen_index(y, team, member):
    return 16 * y + 4 * team + member


TEAMS = [[pen_index(y, q, r) for y in range(2) for r in range(4)] for q in range(4)]
PEERS = [[pen_index(y, q, r) for q in range(4)] for y in range(2) for r in range(4)]


def row_order():
    rows = []
    for y in range(2):
        for r in range(4):
            for q in range(4):
                rows += [CUT * pen_index(y, q, r) + n for n in range(CUT)]
    return np.array(rows)


def split_table(table):
    high = np.asarray(table, dtype=np.float32).astype(jnp.bfloat16)
    low = np.asarray(table - high.astype(np.float64), dtype=np.float32).astype(jnp.bfloat16)
    return np.concatenate([high, low], 0)


@functools.lru_cache(None)
def tables():
    count = NX
    k = np.arange(count)
    angle = 2.0 * np.pi * (np.outer(k, k) % count) / count
    cas = np.cos(angle) + np.sin(angle)
    signed = np.where(k <= count // 2, k, k - count)
    slopes = np.where(k == count // 2, 0, signed)
    slope = slopes[:, None] * (np.cos(angle) - np.sin(angle))
    order = row_order()
    pick = np.ix_(order, order)
    return (
        split_table(cas),
        split_table(slope),
        split_table(cas[pick]),
        split_table(slope[pick].T),
    )


def halves(value):
    high = value.astype(jnp.bfloat16)
    low = (value - high.astype(jnp.float32)).astype(jnp.bfloat16)
    return high, low


def mm(a, b):
    return jnp.dot(a, b, preferred_element_type=jnp.float32)


def times_table(value, table_ref):
    high, low = halves(value)
    n = value.shape[0]
    upper = table_ref[0:NX, :]
    both = mm(jnp.concatenate([high, low], 0), upper)
    return both[0:n] + both[n : 2 * n] + mm(high, table_ref[NX : 2 * NX, :])


def table_times(table_ref, value):
    high, low = halves(value)
    both = mm(table_ref[...], high)
    return both[0:NX] + both[NX : 2 * NX] + mm(table_ref[0:NX, :], low)


def call(kernel, outs, scratch=(), flops=0, moved=0):
    return pl.pallas_call(
        kernel,
        out_shape=outs,
        scratch_shapes=list(scratch),
        cost_estimate=pl.CostEstimate(flops=flops, bytes_accessed=moved, transcendentals=0),
        interpret=INTERPRET,
    )


def f32(*shape):
    return jax.ShapeDtypeStruct(shape, jnp.float32)


def tile(t):
    return slice(TILE * t, TILE * (t + 1))


def gather_rows(state_ref, last_ref, out_ref):
    for q in range(4):
        for member, ref in enumerate((state_ref, last_ref)):
            for t in range(3):
                row = 36 * member + CUT * t
                out_ref[q, row : row + CUT, :] = ref[:, q, tile(t)]


def spread(fields, inverse_ref, cas_ref, slope_ref, send_ref):
    base, tangent = fields
    inverse = inverse_ref[...]
    spectra = jnp.concatenate([base * inverse, tangent * inverse, base, tangent], 0)
    values = times_table(spectra, cas_ref)
    slopes = times_table(spectra, slope_ref)
    for m in range(TEAM):
        cut = slice(WIDE * m, WIDE * (m + 1))
        parts = [values[WIDE * k : WIDE * (k + 1), cut] for k in range(4)]
        parts += [slopes[WIDE * k : WIDE * (k + 1), cut] for k in range(4)]
        block = jnp.concatenate(parts, 1)
        for t in range(3):
            send_ref[m, WIDE * t : WIDE * (t + 1), :] = block[:, tile(t)]


def first_kernel(recv_ref, inverse_ref, cas_ref, slope_ref, send_ref, fields_ref):
    for q in range(4):
        for member in range(2):
            for t in range(3):
                row = 36 * member + CUT * t
                fields_ref[member, CUT * q : CUT * (q + 1), tile(t)] = recv_ref[
                    q, row : row + CUT, :
                ]
    spread((fields_ref[0], fields_ref[1]), inverse_ref, cas_ref, slope_ref, send_ref)


def grid_kernel(recv_ref, cas_ref, slope_ref, send_ref):
    tiles = [
        jnp.concatenate([recv_ref[m, WIDE * t : WIDE * (t + 1), :] for m in range(TEAM)], 0)
        for t in range(3)
    ]
    along_z = table_times(slope_ref, jnp.concatenate(tiles[0:2], 1))
    along_x = table_times(cas_ref, jnp.concatenate(tiles[1:3], 1))
    pair = 2 * WIDE
    psi_z = along_z[:, 0:pair]
    vort_z = along_z[:, pair : 2 * pair]
    psi_x = along_x[:, 64 : 64 + pair]
    vort_x = along_x[:, 64 + pair : 64 + 2 * pair]

    def twice(x):
        return jnp.concatenate([x[:, 0:WIDE], x[:, 0:WIDE]], 1)

    first = psi_x * twice(vort_z) - psi_z * twice(vort_x)
    second = psi_x[:, 0:WIDE] * vort_z[:, WIDE:pair] - psi_z[:, 0:WIDE] * vort_x[:, WIDE:pair]
    zero = jnp.zeros((NZ, WIDE), jnp.float32)
    total = jnp.concatenate([first, jnp.zeros((NZ, TILE - pair), jnp.float32)], 1)
    total = total + jnp.concatenate([zero, second, jnp.zeros((NZ, TILE - pair), jnp.float32)], 1)
    modes = table_times(cas_ref, total)
    for m in range(TEAM):
        send_ref[m] = modes[WIDE * m : WIDE * (m + 1), :]


def advanced(recv_ref, fields_ref, damping_ref, cas_ref):
    lines = [
        jnp.concatenate(
            [recv_ref[m, :, WIDE * member : WIDE * (member + 1)] for m in range(TEAM)], 1
        )
        for member in range(2)
    ]
    forcing = times_table(jnp.concatenate(lines, 0), cas_ref)
    scale = time_step / (NX * NZ)
    damping = damping_ref[...]
    return [
        (fields_ref[member] + scale * forcing[WIDE * member : WIDE * (member + 1)]) * damping
        for member in range(2)
    ]


def middle_kernel(
    recv_ref, old_ref, damping_ref, inverse_ref, cas_ref, slope_ref, send_ref, fields_ref
):
    fields = advanced(recv_ref, old_ref, damping_ref, cas_ref)
    fields_ref[0] = fields[0]
    fields_ref[1] = fields[1]
    spread(fields, inverse_ref, cas_ref, slope_ref, send_ref)


def last_kernel(team_ref, recv_ref, old_ref, damping_ref, cas_ref, *refs):
    outs, keep = refs[:8], refs[8]
    fields = advanced(recv_ref, old_ref, damping_ref, cas_ref)
    for member in range(2):
        for q in range(4):
            for t in range(3):
                keep[member, q, CUT * t : CUT * (t + 1), :] = fields[member][
                    CUT * q : CUT * (q + 1), tile(t)
                ]
    for member in range(2):
        for d in range(4):
            outs[4 * member + d][...] = keep[member, lax.rem(team_ref[0] + d, 4)]


def row_sums(value):
    ones = jnp.ones((8, TILE), jnp.bfloat16)
    first = value.astype(jnp.bfloat16)
    rest = value - first.astype(jnp.float32)
    second = rest.astype(jnp.bfloat16)
    third = (rest - second.astype(jnp.float32)).astype(jnp.bfloat16)
    dims = (((1,), (1,)), ((), ()))
    total = jnp.zeros((8, value.shape[0]), jnp.float32)
    for part in (third, second, first):
        total = total + lax.dot_general(ones, part, dims, preferred_element_type=jnp.float32)
    return total


def fold(value):
    return jnp.sum(value, axis=0, keepdims=True)


def fold(value):
    line = value[:, tile(0)] + value[:, tile(1)] + value[:, tile(2)]
    return jnp.sum(line, axis=0, keepdims=True)


def gram_kernel(kry_ref, out_ref, keep):
    for a in range(0, KRY, 4):
        for b in range(0, a + 1, 4):

            def step(g, sums):
                left = [kry_ref[a + i, g] for i in range(4)]
                right = [kry_ref[b + j, g] for j in range(4)]
                pairs = [(i, j) for i in range(4) for j in range(4)]
                return tuple(sums[4 * i + j] + left[i] * right[j] for i, j in pairs)

            zero = jnp.zeros((PLANES, NX), jnp.float32)
            sums = lax.fori_loop(0, CUT, step, (zero,) * 16)
            for i in range(4):
                for j in range(4):
                    line = fold(sums[4 * i + j])
                    keep[KRY * (a + i) + b + j : KRY * (a + i) + b + j + 1, :] = line
                    if a != b:
                        keep[KRY * (b + j) + a + i : KRY * (b + j) + a + i + 1, :] = line
    packed = row_sums(keep[...])
    row = lax.broadcasted_iota(jnp.int32, (8, TILE), 0)
    out_ref[...] = jnp.where(
        row == 1, packed[:, 0:TILE], jnp.where(row == 2, packed[:, TILE : 2 * TILE], 0.0)
    )


def place(team_ref, parts, out_ref, order):
    for d in range(4):
        order[lax.rem(team_ref[0] + 4 - d, 4)] = parts[d][...]
    for p in range(PLANES):
        for t in range(3):
            out_ref[:, p, tile(t)] = order[p, CUT * t : CUT * (t + 1), :]


def dots_kernel(team_ref, kry_ref, gram_ref, *refs):
    parts, image_ref, out_ref, keep, order = refs[:4], refs[4], refs[5], refs[6], refs[7]
    place(team_ref, parts, image_ref, order)
    image = image_ref[...] - kry_ref[KRY - 1]
    image_ref[...] = image
    keep[...] = jnp.zeros_like(keep)
    for k in range(KRY):
        keep[k : k + 1, :] = fold(jnp.sum(kry_ref[k] * image, axis=0))
    keep[KRY : KRY + 1, :] = fold(jnp.sum(image * image, axis=0))
    packed = row_sums(keep[...])
    row = lax.broadcasted_iota(jnp.int32, (8, TILE), 0)
    out_ref[...] = jnp.where(row == 0, packed, gram_ref[...])


def finish_kernel(team_ref, sums_ref, kry_ref, image_ref, state_ref, *refs):
    parts, residual_ref, next_ref, hess_ref, order = refs[:4], refs[4], refs[5], refs[6], refs[7]
    place(team_ref, parts, residual_ref, order)
    residual_ref[...] = residual_ref[...] - state_ref[...]
    total = float(SEGS * PLANES * NZ * NX)
    sums = sums_ref[0]
    for s in range(1, sums_ref.shape[0]):
        sums = sums + sums_ref[s]
    sums = sums / total
    coeffs = [sums[0:1, k : k + 1] for k in range(KRY)]
    remain = image_ref[...]
    for k in range(KRY):
        remain = remain - coeffs[k] * kry_ref[k]
    lane = lax.broadcasted_iota(jnp.int32, (1, TILE), 1)
    inner = jnp.zeros((1, TILE), jnp.float32)
    outer = [inner, inner]
    for k in range(KRY):
        inner = jnp.where(lane % KRY == k, coeffs[k], inner)
        half, block = k // 8, k % 8
        outer[half] = jnp.where(lane // KRY == block, coeffs[k], outer[half])
    line = jnp.where(lane < KRY, sums[0:1] * sums[0:1], 0.0)
    quadratic = inner * (outer[0] * sums[1:2] + outer[1] * sums[2:3]) - 2.0 * line
    squared = sums[0:1, KRY : KRY + 1] + jnp.sum(quadratic, axis=1, keepdims=True)
    norm = jnp.sqrt(jnp.maximum(squared, 0.0) + 1e-06)
    next_ref[...] = remain / norm
    hess = jnp.where(lane == KRY, norm, sums[0:1])
    hess_ref[...] = jnp.broadcast_to(hess, (8, TILE))


def route(distance, segs):
    pairs = []
    for s in range(segs):
        for y in range(2):
            for q in range(4):
                for r in range(4):
                    here = s * PEN + pen_index(y, q, r)
                    there = (s + 1) % segs * PEN + pen_index(y, (q + distance) % 4, r)
                    pairs.append((here, there))
    return pairs


def gathered(value, axis):
    size = lax.axis_size(axis)
    copies = jnp.broadcast_to(value[None], (size,) + value.shape)
    return lax.all_to_all(copies, axis, 0, 0, tiled=True)


def body(state, krylov):
    pen = lax.axis_index("pen")
    segs = lax.axis_size("seg")
    team = (pen // 4) % 4
    numbers = np.arange(NX)
    signed = np.where(numbers <= NX // 2, numbers, numbers - NX).astype(np.float32)
    steps = np.arange(WIDE)
    rows = CUT * (16 * (pen // 16) + pen % 4) + (4 * CUT * (steps // CUT) + steps % CUT)
    mode = jnp.where(rows <= NZ // 2, rows, rows - NZ).astype(jnp.float32)
    ksquare = mode[:, None] ** 2 + signed[None, :] ** 2
    inverse = jnp.where(ksquare > 0, 1.0 / jnp.where(ksquare > 0, ksquare, 1.0), 0.0)
    damping = 1.0 / (1.0 + time_step * viscosity * ksquare)
    cas, slope, cas_z, slope_z = [jnp.asarray(t) for t in tables()]
    team_ref = team.astype(jnp.int32).reshape(1)
    smem = pl.BlockSpec(memory_space=pltpu.SMEM)
    vmem = pl.BlockSpec(memory_space=pltpu.VMEM)

    state_f = state.transpose(1, 0, 2)
    kry_f = krylov.transpose(0, 2, 1, 3)
    exchange = functools.partial(
        lax.all_to_all, axis_name="pen", split_axis=0, concat_axis=0, tiled=True
    )

    whole = pl.BlockSpec((CUT, PLANES, NX), lambda i: (0, 0, 0))
    last = pl.BlockSpec((None, CUT, PLANES, NX), lambda i: (KRY - 1, 0, 0, 0))
    packed = pl.pallas_call(
        gather_rows,
        grid=(1,),
        in_specs=[whole, last],
        out_specs=pl.BlockSpec((4, 72, TILE), lambda i: (0, 0, 0)),
        out_shape=f32(4, 72, TILE),
        interpret=INTERPRET,
    )(state_f, kry_f)
    packed = exchange(packed, axis_index_groups=PEERS)
    gram = call(
        gram_kernel,
        f32(8, TILE),
        [pltpu.VMEM((KRY * KRY, TILE), jnp.float32)],
        flops=10_000_000,
        moved=1_300_000,
    )(kry_f)
    send, fields = call(
        first_kernel, (f32(TEAM, 144, TILE), f32(2, WIDE, NX)), flops=700_000_000, moved=3_000_000
    )(packed, inverse, cas, slope)
    for repeat in range(STEPS):
        recv = exchange(send, axis_index_groups=TEAMS)
        modes = call(
            grid_kernel, f32(TEAM, WIDE, TILE), flops=900_000_000, moved=2_500_000
        )(recv, cas_z, slope_z)
        recv = exchange(modes, axis_index_groups=TEAMS)
        if repeat < STEPS - 1:
            send, fields = call(
                middle_kernel,
                (f32(TEAM, 144, TILE), f32(2, WIDE, NX)),
                flops=900_000_000,
                moved=3_000_000,
            )(recv, fields, damping, inverse, cas, slope)
    pieces = pl.pallas_call(
        last_kernel,
        in_specs=[smem] + [vmem] * 4,
        out_specs=[vmem] * 8,
        out_shape=[f32(36, TILE)] * 8,
        scratch_shapes=[pltpu.VMEM((2, 4, 36, TILE), jnp.float32)],
        cost_estimate=pl.CostEstimate(flops=200_000_000, bytes_accessed=1_500_000, transcendentals=0),
        interpret=INTERPRET,
    )(team_ref, recv, fields, damping, cas)
    tangent = [lax.ppermute(pieces[4 + d], ("seg", "pen"), route(d, segs)) for d in range(4)]
    base = [lax.ppermute(pieces[d], ("seg", "pen"), route(d, segs)) for d in range(4)]
    image, partial = pl.pallas_call(
        dots_kernel,
        in_specs=[smem] + [vmem] * 6,
        out_specs=[vmem] * 2,
        out_shape=[f32(CUT, PLANES, NX), f32(8, TILE)],
        scratch_shapes=[
            pltpu.VMEM((TILE, TILE), jnp.float32),
            pltpu.VMEM((4, 36, TILE), jnp.float32),
        ],
        cost_estimate=pl.CostEstimate(flops=1_000_000, bytes_accessed=1_300_000, transcendentals=0),
        interpret=INTERPRET,
    )(team_ref, kry_f, gram, *tangent)
    sums = gathered(partial, "pen")
    sums = gathered(jnp.sum(sums, axis=0), "seg")
    residual, vector, hess = pl.pallas_call(
        finish_kernel,
        in_specs=[smem] + [vmem] * 8,
        out_specs=[vmem] * 3,
        out_shape=[f32(CUT, PLANES, NX)] * 2 + [f32(8, TILE)],
        scratch_shapes=[pltpu.VMEM((4, 36, TILE), jnp.float32)],
        cost_estimate=pl.CostEstimate(flops=1_000_000, bytes_accessed=1_500_000, transcendentals=0),
        interpret=INTERPRET,
    )(team_ref, sums, kry_f, image, state_f, *base)
    return (residual.transpose(1, 0, 2), vector.transpose(1, 0, 2), hess[0, : KRY + 1])


def solution(mesh):
    return jax.shard_map(
        body,
        mesh=mesh,
        in_specs=(P("seg", "pen", None), P(None, "seg", "pen", None)),
        out_specs=(P("seg", "pen", None), P("seg", "pen", None), P()),
        check_vma=False,
    )
```

```python
import functools

import jax
import jax.numpy as jnp
import numpy as np
from jax import lax
from jax.experimental import pallas as pl
from jax.experimental.pallas import tpu as pltpu
from jax.sharding import PartitionSpec as P

NX = 384
NZ = 384
PLANES = 4
STEPS = 2
KRY = 16
SEGS = 16
PEN = 32
CUT = NZ // PEN
TEAM = 8
WIDE = NZ // TEAM
TILE = 128
INTERPRET = False

time_step = 0.0003
viscosity = 0.0226


def pen_index(y, team, member):
    return 16 * y + 4 * team + member


TEAMS = [[pen_index(y, q, r) for y in range(2) for r in range(4)] for q in range(4)]
PEERS = [[pen_index(y, q, r) for q in range(4)] for y in range(2) for r in range(4)]


def row_order():
    rows = []
    for y in range(2):
        for r in range(4):
            for q in range(4):
                rows += [CUT * pen_index(y, q, r) + n for n in range(CUT)]
    return np.array(rows)


def split_table(table):
    high = np.asarray(table, dtype=np.float32).astype(jnp.bfloat16)
    low = np.asarray(table - high.astype(np.float64), dtype=np.float32).astype(jnp.bfloat16)
    return np.concatenate([high, low], 0)


@functools.lru_cache(None)
def tables():
    count = NX
    k = np.arange(count)
    angle = 2.0 * np.pi * (np.outer(k, k) % count) / count
    cas = np.cos(angle) + np.sin(angle)
    signed = np.where(k <= count // 2, k, k - count)
    slopes = np.where(k == count // 2, 0, signed)
    slope = slopes[:, None] * (np.cos(angle) - np.sin(angle))
    order = row_order()
    pick = np.ix_(order, order)
    return (
        split_table(cas),
        split_table(slope),
        split_table(cas[pick]),
        split_table(slope[pick].T),
    )


def halves(value):
    high = value.astype(jnp.bfloat16)
    low = (value - high.astype(jnp.float32)).astype(jnp.bfloat16)
    return high, low


def mm(a, b):
    return jnp.dot(a, b, preferred_element_type=jnp.float32)


def times_table(value, table_ref):
    high, low = halves(value)
    n = value.shape[0]
    upper = table_ref[0:NX, :]
    both = mm(jnp.concatenate([high, low], 0), upper)
    return both[0:n] + both[n : 2 * n] + mm(high, table_ref[NX : 2 * NX, :])


def table_times(table_ref, value):
    high, low = halves(value)
    both = mm(table_ref[...], high)
    return both[0:NX] + both[NX : 2 * NX] + mm(table_ref[0:NX, :], low)


def call(kernel, outs, operands, scratch=(), flops=0, moved=0, keep=True):
    vmem = pl.BlockSpec(memory_space=pltpu.VMEM)
    single = not isinstance(outs, (list, tuple))
    shapes = [outs] if single else list(outs)
    if not INTERPRET:
        operands = [pltpu.with_memory_space_constraint(x, pltpu.VMEM) for x in operands]
        shapes = [pltpu.VMEM(x.shape, x.dtype) for x in shapes] if keep else shapes
    results = pl.pallas_call(
        kernel,
        in_specs=[vmem] * len(operands),
        out_specs=[vmem] * len(shapes),
        out_shape=shapes,
        scratch_shapes=list(scratch),
        cost_estimate=pl.CostEstimate(flops=flops, bytes_accessed=moved, transcendentals=0),
        compiler_params=pltpu.CompilerParams(vmem_limit_bytes=24 << 20),
        interpret=INTERPRET,
    )(*operands)
    return results[0] if single else results


def f32(*shape):
    return jax.ShapeDtypeStruct(shape, jnp.float32)


def tile(t):
    return slice(TILE * t, TILE * (t + 1))


def gather_rows(state_ref, last_ref, out_ref):
    for q in range(4):
        for member, ref in enumerate((state_ref, last_ref)):
            for t in range(3):
                row = 36 * member + CUT * t
                out_ref[q, row : row + CUT, :] = ref[:, q, tile(t)]


def spread(fields, inverse_ref, cas_ref, slope_ref, send_ref):
    base, tangent = fields
    inverse = inverse_ref[...]
    spectra = jnp.concatenate([base * inverse, tangent * inverse, base, tangent], 0)
    values = times_table(spectra, cas_ref)
    slopes = times_table(spectra, slope_ref)
    for m in range(TEAM):
        cut = slice(WIDE * m, WIDE * (m + 1))
        parts = [values[WIDE * k : WIDE * (k + 1), cut] for k in range(4)]
        parts += [slopes[WIDE * k : WIDE * (k + 1), cut] for k in range(4)]
        block = jnp.concatenate(parts, 1)
        for t in range(3):
            send_ref[m, WIDE * t : WIDE * (t + 1), :] = block[:, tile(t)]


def first_kernel(recv_ref, inverse_ref, cas_ref, slope_ref, send_ref, fields_ref):
    for q in range(4):
        for member in range(2):
            for t in range(3):
                row = 36 * member + CUT * t
                fields_ref[member, CUT * q : CUT * (q + 1), tile(t)] = recv_ref[
                    q, row : row + CUT, :
                ]
    spread((fields_ref[0], fields_ref[1]), inverse_ref, cas_ref, slope_ref, send_ref)


def grid_kernel(recv_ref, cas_ref, slope_ref, send_ref):
    tiles = [
        jnp.concatenate([recv_ref[m, WIDE * t : WIDE * (t + 1), :] for m in range(TEAM)], 0)
        for t in range(3)
    ]
    along_z = table_times(slope_ref, jnp.concatenate(tiles[0:2], 1))
    along_x = table_times(cas_ref, jnp.concatenate(tiles[1:3], 1))
    pair = 2 * WIDE
    psi_z = along_z[:, 0:pair]
    vort_z = along_z[:, pair : 2 * pair]
    psi_x = along_x[:, 64 : 64 + pair]
    vort_x = along_x[:, 64 + pair : 64 + 2 * pair]

    def twice(x):
        return jnp.concatenate([x[:, 0:WIDE], x[:, 0:WIDE]], 1)

    first = psi_x * twice(vort_z) - psi_z * twice(vort_x)
    second = psi_x[:, 0:WIDE] * vort_z[:, WIDE:pair] - psi_z[:, 0:WIDE] * vort_x[:, WIDE:pair]
    zero = jnp.zeros((NZ, WIDE), jnp.float32)
    total = jnp.concatenate([first, jnp.zeros((NZ, TILE - pair), jnp.float32)], 1)
    total = total + jnp.concatenate([zero, second, jnp.zeros((NZ, TILE - pair), jnp.float32)], 1)
    modes = table_times(cas_ref, total)
    for m in range(TEAM):
        send_ref[m] = modes[WIDE * m : WIDE * (m + 1), :]


def advanced(recv_ref, fields_ref, damping_ref, cas_ref):
    lines = [
        jnp.concatenate(
            [recv_ref[m, :, WIDE * member : WIDE * (member + 1)] for m in range(TEAM)], 1
        )
        for member in range(2)
    ]
    forcing = times_table(jnp.concatenate(lines, 0), cas_ref)
    scale = time_step / (NX * NZ)
    damping = damping_ref[...]
    return [
        (fields_ref[member] + scale * forcing[WIDE * member : WIDE * (member + 1)]) * damping
        for member in range(2)
    ]


def middle_kernel(
    recv_ref, old_ref, damping_ref, inverse_ref, cas_ref, slope_ref, send_ref, fields_ref
):
    fields = advanced(recv_ref, old_ref, damping_ref, cas_ref)
    fields_ref[0] = fields[0]
    fields_ref[1] = fields[1]
    spread(fields, inverse_ref, cas_ref, slope_ref, send_ref)


def last_kernel(recv_ref, old_ref, damping_ref, cas_ref, out_ref):
    fields = advanced(recv_ref, old_ref, damping_ref, cas_ref)
    for member in range(2):
        for q in range(4):
            for t in range(3):
                row = 36 * member + CUT * t
                out_ref[q, row : row + CUT, :] = fields[member][
                    CUT * q : CUT * (q + 1), tile(t)
                ]


def row_sums(value):
    ones = jnp.ones((8, TILE), jnp.bfloat16)
    first = value.astype(jnp.bfloat16)
    rest = value - first.astype(jnp.float32)
    second = rest.astype(jnp.bfloat16)
    third = (rest - second.astype(jnp.float32)).astype(jnp.bfloat16)
    dims = (((1,), (1,)), ((), ()))
    total = jnp.zeros((8, value.shape[0]), jnp.float32)
    for part in (third, second, first):
        total = total + lax.dot_general(ones, part, dims, preferred_element_type=jnp.float32)
    return total


def fold(value):
    return jnp.sum(value, axis=0, keepdims=True)


def fold(value):
    line = value[:, tile(0)] + value[:, tile(1)] + value[:, tile(2)]
    return jnp.sum(line, axis=0, keepdims=True)


def gram_kernel(kry_ref, out_ref, keep):
    for a in range(0, KRY, 4):
        for b in range(0, a + 1, 4):

            def step(g, sums):
                left = [kry_ref[a + i, g] for i in range(4)]
                right = [kry_ref[b + j, g] for j in range(4)]
                pairs = [(i, j) for i in range(4) for j in range(4)]
                return tuple(sums[4 * i + j] + left[i] * right[j] for i, j in pairs)

            zero = jnp.zeros((PLANES, NX), jnp.float32)
            sums = lax.fori_loop(0, CUT, step, (zero,) * 16)
            for i in range(4):
                for j in range(4):
                    line = fold(sums[4 * i + j])
                    keep[KRY * (a + i) + b + j : KRY * (a + i) + b + j + 1, :] = line
                    if a != b:
                        keep[KRY * (b + j) + a + i : KRY * (b + j) + a + i + 1, :] = line
    packed = row_sums(keep[...])
    row = lax.broadcasted_iota(jnp.int32, (8, TILE), 0)
    out_ref[...] = jnp.where(
        row == 1, packed[:, 0:TILE], jnp.where(row == 2, packed[:, TILE : 2 * TILE], 0.0)
    )


def place(planes_ref, out_ref):
    for p in range(PLANES):
        for t in range(3):
            out_ref[:, p, tile(t)] = planes_ref[p, CUT * t : CUT * (t + 1), :]


def dots_kernel(planes_ref, kry_ref, gram_ref, image_ref, out_ref, keep):
    place(planes_ref, image_ref)
    image = image_ref[...] - kry_ref[KRY - 1]
    image_ref[...] = image
    keep[...] = jnp.zeros_like(keep)
    for k in range(KRY):
        keep[k : k + 1, :] = fold(jnp.sum(kry_ref[k] * image, axis=0))
    keep[KRY : KRY + 1, :] = fold(jnp.sum(image * image, axis=0))
    packed = row_sums(keep[...])
    row = lax.broadcasted_iota(jnp.int32, (8, TILE), 0)
    sums = jnp.where(row == 0, packed, gram_ref[...])
    for m in range(out_ref.shape[0]):
        out_ref[m] = sums


def finish_kernel(
    sums_ref, kry_ref, image_ref, state_ref, planes_ref, residual_ref, next_ref, hess_ref
):
    place(planes_ref, residual_ref)
    residual_ref[...] = residual_ref[...] - state_ref[...]
    total = float(SEGS * PLANES * NZ * NX)
    sums = sums_ref[0]
    for s in range(1, sums_ref.shape[0]):
        sums = sums + sums_ref[s]
    sums = sums / total
    coeffs = [sums[0:1, k : k + 1] for k in range(KRY)]
    remain = image_ref[...]
    for k in range(KRY):
        remain = remain - coeffs[k] * kry_ref[k]
    lane = lax.broadcasted_iota(jnp.int32, (1, TILE), 1)
    inner = jnp.zeros((1, TILE), jnp.float32)
    outer = [inner, inner]
    for k in range(KRY):
        inner = jnp.where(lane % KRY == k, coeffs[k], inner)
        half, block = k // 8, k % 8
        outer[half] = jnp.where(lane // KRY == block, coeffs[k], outer[half])
    line = jnp.where(lane < KRY, sums[0:1] * sums[0:1], 0.0)
    quadratic = inner * (outer[0] * sums[1:2] + outer[1] * sums[2:3]) - 2.0 * line
    squared = sums[0:1, KRY : KRY + 1] + jnp.sum(quadratic, axis=1, keepdims=True)
    norm = jnp.sqrt(jnp.maximum(squared, 0.0) + 1e-06)
    next_ref[...] = remain / norm
    hess = jnp.where(lane == KRY, norm, sums[0:1])
    hess_ref[...] = hess[0, : KRY + 1]


def body(state, krylov):
    pen = lax.axis_index("pen")
    segs = lax.axis_size("seg")
    numbers = np.arange(NX)
    signed = np.where(numbers <= NX // 2, numbers, numbers - NX).astype(np.float32)
    steps = np.arange(WIDE)
    rows = CUT * (16 * (pen // 16) + pen % 4) + (4 * CUT * (steps // CUT) + steps % CUT)
    mode = jnp.where(rows <= NZ // 2, rows, rows - NZ).astype(jnp.float32)
    ksquare = mode[:, None] ** 2 + signed[None, :] ** 2
    inverse = jnp.where(ksquare > 0, 1.0 / jnp.where(ksquare > 0, ksquare, 1.0), 0.0)
    damping = 1.0 / (1.0 + time_step * viscosity * ksquare)
    cas, slope, cas_z, slope_z = [jnp.asarray(t) for t in tables()]
    state_f = state.transpose(1, 0, 2)
    kry_f = krylov.transpose(0, 2, 1, 3)
    exchange = functools.partial(
        lax.all_to_all, axis_name="pen", split_axis=0, concat_axis=0, tiled=True
    )
    ring = [(s, (s + 1) % segs) for s in range(segs)]

    whole = pl.BlockSpec((CUT, PLANES, NX), lambda i: (0, 0, 0))
    last = pl.BlockSpec((None, CUT, PLANES, NX), lambda i: (KRY - 1, 0, 0, 0))
    inputs = [state_f, kry_f]
    if not INTERPRET:
        inputs = [pltpu.with_memory_space_constraint(x, pltpu.HBM) for x in inputs]
    packed = pl.pallas_call(
        gather_rows,
        grid=(1,),
        in_specs=[whole, last],
        out_specs=pl.BlockSpec((4, 72, TILE), lambda i: (0, 0, 0)),
        out_shape=f32(4, 72, TILE),
        compiler_params=pltpu.CompilerParams(vmem_limit_bytes=24 << 20),
        interpret=INTERPRET,
    )(*inputs)
    packed = exchange(packed, axis_index_groups=PEERS)
    gram = call(
        gram_kernel,
        f32(8, TILE),
        [kry_f],
        [pltpu.VMEM((KRY * KRY, TILE), jnp.float32)],
        flops=10_000_000,
        moved=1_300_000,
    )
    packed, gram = lax.optimization_barrier((packed, gram))
    both = (f32(TEAM, 144, TILE), f32(2, WIDE, NX))
    send, fields = call(
        first_kernel, both, [packed, inverse, cas, slope], flops=700_000_000, moved=3_000_000
    )
    for repeat in range(STEPS):
        recv = exchange(send, axis_index_groups=TEAMS)
        modes = call(
            grid_kernel,
            f32(TEAM, WIDE, TILE),
            [recv, cas_z, slope_z],
            flops=900_000_000,
            moved=2_500_000,
        )
        recv = exchange(modes, axis_index_groups=TEAMS)
        if repeat < STEPS - 1:
            send, fields = call(
                middle_kernel,
                both,
                [recv, fields, damping, inverse, cas, slope],
                flops=900_000_000,
                moved=3_000_000,
            )
    ends = call(
        last_kernel,
        f32(4, 72, TILE),
        [recv, fields, damping, cas],
        flops=200_000_000,
        moved=1_500_000,
    )
    ends = exchange(ends, axis_index_groups=PEERS)
    tangent = lax.ppermute(ends[:, 36:72], "seg", ring)
    base = lax.ppermute(ends[:, 0:36], "seg", ring)
    image, partial = call(
        dots_kernel,
        [f32(CUT, PLANES, NX), f32(PEN, 8, TILE)],
        [tangent, kry_f, gram],
        [pltpu.VMEM((TILE, TILE), jnp.float32)],
        flops=1_000_000,
        moved=1_300_000,
    )
    sums = jnp.sum(exchange(partial), axis=0)
    sums = jnp.broadcast_to(sums[None], (segs, 8, TILE))
    sums = lax.all_to_all(sums, "seg", 0, 0, tiled=True)
    residual, vector, hess = call(
        finish_kernel,
        [f32(CUT, PLANES, NX)] * 2 + [f32(KRY + 1)],
        [sums, kry_f, image, state_f, base],
        flops=1_000_000,
        moved=1_500_000,
        keep=False,
    )
    return (residual.transpose(1, 0, 2), vector.transpose(1, 0, 2), hess)


def solution(mesh):
    return jax.shard_map(
        body,
        mesh=mesh,
        in_specs=(P("seg", "pen", None), P(None, "seg", "pen", None)),
        out_specs=(P("seg", "pen", None), P("seg", "pen", None), P()),
        check_vma=False,
    )
```

```python
import functools

import jax
import jax.numpy as jnp
import numpy as np
from jax import lax
from jax.experimental import pallas as pl
from jax.experimental.pallas import tpu as pltpu
from jax.sharding import PartitionSpec as P


NX = 384
NZ = 384
PLANES = 4
STEPS = 2
KRY = 16
SEGS = 16
PEN = 32
CUT = NZ // PEN
TEAM = 8
WIDE = NZ // TEAM
TILE = 128
INTERPRET = False

time_step = 0.0003
viscosity = 0.0226


def pen_index(y, team, member):
    return 16 * y + 4 * team + member


TEAMS = [[pen_index(y, q, r) for y in range(2) for r in range(4)] for q in range(4)]
PEERS = [[pen_index(y, q, r) for q in range(4)] for y in range(2) for r in range(4)]


def row_order():
    rows = []
    for y in range(2):
        for r in range(4):
            for q in range(4):
                rows += [CUT * pen_index(y, q, r) + n for n in range(CUT)]
    return np.array(rows)


def split_table(table):
    high = np.asarray(table, dtype=np.float32).astype(jnp.bfloat16)
    low = np.asarray(table - high.astype(np.float64), dtype=np.float32).astype(jnp.bfloat16)
    return np.concatenate([high, low], 0)


@functools.lru_cache(None)
def tables():
    count = NX
    k = np.arange(count)
    angle = 2.0 * np.pi * (np.outer(k, k) % count) / count
    cas = np.cos(angle) + np.sin(angle)
    signed = np.where(k <= count // 2, k, k - count)
    slopes = np.where(k == count // 2, 0, signed)
    slope = slopes[:, None] * (np.cos(angle) - np.sin(angle))
    order = row_order()
    pick = np.ix_(order, order)
    return (
        split_table(cas),
        split_table(slope),
        split_table(cas[pick]),
        split_table(slope[pick].T),
    )


def halves(value):
    high = value.astype(jnp.bfloat16)
    low = (value - high.astype(jnp.float32)).astype(jnp.bfloat16)
    return high, low


def mm(a, b):
    return jnp.dot(a, b, preferred_element_type=jnp.float32)


def times_table(value, table_ref):
    high, low = halves(value)
    n = value.shape[0]
    upper = table_ref[0:NX, :]
    both = mm(jnp.concatenate([high, low], 0), upper)
    return both[0:n] + both[n : 2 * n] + mm(high, table_ref[NX : 2 * NX, :])


def table_times(table_ref, value):
    high, low = halves(value)
    both = mm(table_ref[...], high)
    return both[0:NX] + both[NX : 2 * NX] + mm(table_ref[0:NX, :], low)


def call(kernel, outs, operands, scratch=(), flops=0, moved=0, keep=True):
    vmem = pl.BlockSpec(memory_space=pltpu.VMEM)
    single = not isinstance(outs, (list, tuple))
    shapes = [outs] if single else list(outs)
    if not INTERPRET:
        operands = [pltpu.with_memory_space_constraint(x, pltpu.VMEM) for x in operands]
        shapes = [pltpu.VMEM(x.shape, x.dtype) for x in shapes] if keep else shapes
    results = pl.pallas_call(
        kernel,
        in_specs=[vmem] * len(operands),
        out_specs=[vmem] * len(shapes),
        out_shape=shapes,
        scratch_shapes=list(scratch),
        cost_estimate=pl.CostEstimate(flops=flops, bytes_accessed=moved, transcendentals=0),
        compiler_params=pltpu.CompilerParams(vmem_limit_bytes=24 << 20),
        interpret=INTERPRET,
    )(*operands)
    return results[0] if single else results


def f32(*shape):
    return jax.ShapeDtypeStruct(shape, jnp.float32)


def tile(t):
    return slice(TILE * t, TILE * (t + 1))


def gather_rows(state_ref, last_ref, out_ref):
    for q in range(4):
        for member, ref in enumerate((state_ref, last_ref)):
            for t in range(3):
                row = 36 * member + CUT * t
                out_ref[q, row : row + CUT, :] = ref[:, q, tile(t)]


def spread(fields, inverse_ref, cas_ref, slope_ref, send_ref):
    base, tangent = fields
    inverse = inverse_ref[...]
    spectra = jnp.concatenate([base * inverse, tangent * inverse, base, tangent], 0)
    values = times_table(spectra, cas_ref)
    slopes = times_table(spectra, slope_ref)
    for m in range(TEAM):
        cut = slice(WIDE * m, WIDE * (m + 1))
        parts = [values[WIDE * k : WIDE * (k + 1), cut] for k in range(4)]
        parts += [slopes[WIDE * k : WIDE * (k + 1), cut] for k in range(4)]
        block = jnp.concatenate(parts, 1)
        for t in range(3):
            send_ref[m, WIDE * t : WIDE * (t + 1), :] = block[:, tile(t)]


def first_kernel(recv_ref, inverse_ref, cas_ref, slope_ref, send_ref, fields_ref):
    for q in range(4):
        for member in range(2):
            for t in range(3):
                row = 36 * member + CUT * t
                fields_ref[member, CUT * q : CUT * (q + 1), tile(t)] = recv_ref[
                    q, row : row + CUT, :
                ]
    spread((fields_ref[0], fields_ref[1]), inverse_ref, cas_ref, slope_ref, send_ref)


def grid_kernel(recv_ref, cas_ref, slope_ref, send_ref):
    tiles = [
        jnp.concatenate([recv_ref[m, WIDE * t : WIDE * (t + 1), :] for m in range(TEAM)], 0)
        for t in range(3)
    ]
    along_z = table_times(slope_ref, jnp.concatenate(tiles[0:2], 1))
    along_x = table_times(cas_ref, jnp.concatenate(tiles[1:3], 1))
    pair = 2 * WIDE
    psi_z = along_z[:, 0:pair]
    vort_z = along_z[:, pair : 2 * pair]
    psi_x = along_x[:, 64 : 64 + pair]
    vort_x = along_x[:, 64 + pair : 64 + 2 * pair]

    def twice(x):
        return jnp.concatenate([x[:, 0:WIDE], x[:, 0:WIDE]], 1)

    first = psi_x * twice(vort_z) - psi_z * twice(vort_x)
    second = psi_x[:, 0:WIDE] * vort_z[:, WIDE:pair] - psi_z[:, 0:WIDE] * vort_x[:, WIDE:pair]
    zero = jnp.zeros((NZ, WIDE), jnp.float32)
    total = jnp.concatenate([first, jnp.zeros((NZ, TILE - pair), jnp.float32)], 1)
    total = total + jnp.concatenate([zero, second, jnp.zeros((NZ, TILE - pair), jnp.float32)], 1)
    modes = table_times(cas_ref, total)
    for m in range(TEAM):
        send_ref[m] = modes[WIDE * m : WIDE * (m + 1), :]


def advanced(recv_ref, fields_ref, damping_ref, cas_ref):
    lines = [
        jnp.concatenate(
            [recv_ref[m, :, WIDE * member : WIDE * (member + 1)] for m in range(TEAM)], 1
        )
        for member in range(2)
    ]
    forcing = times_table(jnp.concatenate(lines, 0), cas_ref)
    scale = time_step / (NX * NZ)
    damping = damping_ref[...]
    return [
        (fields_ref[member] + scale * forcing[WIDE * member : WIDE * (member + 1)]) * damping
        for member in range(2)
    ]


def middle_kernel(
    recv_ref, old_ref, damping_ref, inverse_ref, cas_ref, slope_ref, send_ref, fields_ref
):
    fields = advanced(recv_ref, old_ref, damping_ref, cas_ref)
    fields_ref[0] = fields[0]
    fields_ref[1] = fields[1]
    spread(fields, inverse_ref, cas_ref, slope_ref, send_ref)


def last_kernel(recv_ref, old_ref, damping_ref, cas_ref, out_ref):
    fields = advanced(recv_ref, old_ref, damping_ref, cas_ref)
    for member in range(2):
        for q in range(4):
            for t in range(3):
                row = 36 * member + CUT * t
                out_ref[q, row : row + CUT, :] = fields[member][
                    CUT * q : CUT * (q + 1), tile(t)
                ]


def row_sums(value):
    ones = jnp.ones((8, TILE), jnp.bfloat16)
    first = value.astype(jnp.bfloat16)
    rest = value - first.astype(jnp.float32)
    second = rest.astype(jnp.bfloat16)
    third = (rest - second.astype(jnp.float32)).astype(jnp.bfloat16)
    dims = (((1,), (1,)), ((), ()))
    total = jnp.zeros((8, value.shape[0]), jnp.float32)
    for part in (third, second, first):
        total = total + lax.dot_general(ones, part, dims, preferred_element_type=jnp.float32)
    return total


def fold(value):
    return jnp.sum(value, axis=0, keepdims=True)


def fold(value):
    line = value[:, tile(0)] + value[:, tile(1)] + value[:, tile(2)]
    return jnp.sum(line, axis=0, keepdims=True)


def gram_kernel(kry_ref, out_ref, keep):
    for a in range(0, KRY, 4):
        for b in range(0, a + 1, 4):

            def step(g, sums):
                left = [kry_ref[a + i, g] for i in range(4)]
                right = [kry_ref[b + j, g] for j in range(4)]
                pairs = [(i, j) for i in range(4) for j in range(4)]
                return tuple(sums[4 * i + j] + left[i] * right[j] for i, j in pairs)

            zero = jnp.zeros((PLANES, NX), jnp.float32)
            sums = lax.fori_loop(0, CUT, step, (zero,) * 16)
            for i in range(4):
                for j in range(4):
                    line = fold(sums[4 * i + j])
                    keep[KRY * (a + i) + b + j : KRY * (a + i) + b + j + 1, :] = line
                    if a != b:
                        keep[KRY * (b + j) + a + i : KRY * (b + j) + a + i + 1, :] = line
    packed = row_sums(keep[...])
    row = lax.broadcasted_iota(jnp.int32, (8, TILE), 0)
    out_ref[...] = jnp.where(
        row == 1, packed[:, 0:TILE], jnp.where(row == 2, packed[:, TILE : 2 * TILE], 0.0)
    )


def place(planes_ref, out_ref):
    for p in range(PLANES):
        for t in range(3):
            out_ref[:, p, tile(t)] = planes_ref[p, CUT * t : CUT * (t + 1), :]


def dots_kernel(planes_ref, kry_ref, gram_ref, image_ref, out_ref, keep):
    place(planes_ref, image_ref)
    image = image_ref[...] - kry_ref[KRY - 1]
    image_ref[...] = image
    keep[...] = jnp.zeros_like(keep)
    for k in range(KRY):
        keep[k : k + 1, :] = fold(jnp.sum(kry_ref[k] * image, axis=0))
    keep[KRY : KRY + 1, :] = fold(jnp.sum(image * image, axis=0))
    packed = row_sums(keep[...])
    row = lax.broadcasted_iota(jnp.int32, (8, TILE), 0)
    sums = jnp.where(row == 0, packed, gram_ref[...])
    for m in range(out_ref.shape[0]):
        out_ref[m] = sums


def finish_kernel(
    sums_ref, kry_ref, image_ref, state_ref, planes_ref, residual_ref, next_ref, hess_ref
):
    place(planes_ref, residual_ref)
    residual_ref[...] = residual_ref[...] - state_ref[...]
    total = float(SEGS * PLANES * NZ * NX)
    sums = sums_ref[0]
    for s in range(1, sums_ref.shape[0]):
        sums = sums + sums_ref[s]
    sums = sums / total
    coeffs = [sums[0:1, k : k + 1] for k in range(KRY)]
    remain = image_ref[...]
    for k in range(KRY):
        remain = remain - coeffs[k] * kry_ref[k]
    lane = lax.broadcasted_iota(jnp.int32, (1, TILE), 1)
    inner = jnp.zeros((1, TILE), jnp.float32)
    outer = [inner, inner]
    for k in range(KRY):
        inner = jnp.where(lane % KRY == k, coeffs[k], inner)
        half, block = k // 8, k % 8
        outer[half] = jnp.where(lane // KRY == block, coeffs[k], outer[half])
    line = jnp.where(lane < KRY, sums[0:1] * sums[0:1], 0.0)
    quadratic = inner * (outer[0] * sums[1:2] + outer[1] * sums[2:3]) - 2.0 * line
    squared = sums[0:1, KRY : KRY + 1] + jnp.sum(quadratic, axis=1, keepdims=True)
    norm = jnp.sqrt(jnp.maximum(squared, 0.0) + 1e-06)
    next_ref[...] = remain / norm
    hess = jnp.where(lane == KRY, norm, sums[0:1])
    hess_ref[...] = hess[0, : KRY + 1]


def reduce_groups(segs):
    def number(place, inner):
        seg, y = place
        return seg * PEN + 16 * y + inner

    places = [(seg, y) for seg in range(segs) for y in range(2)]
    columns = [[number(place, inner) for inner in range(16)] for place in places]
    planes = [[number(place, inner) for place in places] for inner in range(16)]
    return columns, planes


def body(state, krylov):
    pen = lax.axis_index("pen")
    segs = lax.axis_size("seg")
    numbers = np.arange(NX)
    signed = np.where(numbers <= NX // 2, numbers, numbers - NX).astype(np.float32)
    steps = np.arange(WIDE)
    rows = CUT * (16 * (pen // 16) + pen % 4) + (4 * CUT * (steps // CUT) + steps % CUT)
    mode = jnp.where(rows <= NZ // 2, rows, rows - NZ).astype(jnp.float32)
    ksquare = mode[:, None] ** 2 + signed[None, :] ** 2
    inverse = jnp.where(ksquare > 0, 1.0 / jnp.where(ksquare > 0, ksquare, 1.0), 0.0)
    damping = 1.0 / (1.0 + time_step * viscosity * ksquare)
    cas, slope, cas_z, slope_z = [jnp.asarray(t) for t in tables()]
    state_f = state.transpose(1, 0, 2)
    kry_f = krylov.transpose(0, 2, 1, 3)
    exchange = functools.partial(
        lax.all_to_all, axis_name="pen", split_axis=0, concat_axis=0, tiled=True
    )
    everywhere = functools.partial(
        lax.all_to_all, axis_name=("seg", "pen"), split_axis=0, concat_axis=0, tiled=True
    )
    columns, planes = reduce_groups(segs)
    ring = [(s, (s + 1) % segs) for s in range(segs)]

    whole = pl.BlockSpec((CUT, PLANES, NX), lambda i: (0, 0, 0))
    last = pl.BlockSpec((None, CUT, PLANES, NX), lambda i: (KRY - 1, 0, 0, 0))
    inputs = [state_f, kry_f]
    if not INTERPRET:
        inputs = [pltpu.with_memory_space_constraint(x, pltpu.HBM) for x in inputs]
    packed = pl.pallas_call(
        gather_rows,
        grid=(1,),
        in_specs=[whole, last],
        out_specs=pl.BlockSpec((4, 72, TILE), lambda i: (0, 0, 0)),
        out_shape=f32(4, 72, TILE),
        compiler_params=pltpu.CompilerParams(vmem_limit_bytes=24 << 20),
        interpret=INTERPRET,
    )(*inputs)
    packed = exchange(packed, axis_index_groups=PEERS)
    gram = call(
        gram_kernel,
        f32(8, TILE),
        [kry_f],
        [pltpu.VMEM((KRY * KRY, TILE), jnp.float32)],
        flops=10_000_000,
        moved=1_300_000,
    )
    packed, gram = lax.optimization_barrier((packed, gram))
    both = (f32(TEAM, 144, TILE), f32(2, WIDE, NX))
    send, fields = call(
        first_kernel, both, [packed, inverse, cas, slope], flops=700_000_000, moved=3_000_000
    )
    for repeat in range(STEPS):
        recv = exchange(send, axis_index_groups=TEAMS)
        modes = call(
            grid_kernel,
            f32(TEAM, WIDE, TILE),
            [recv, cas_z, slope_z],
            flops=900_000_000,
            moved=2_500_000,
        )
        recv = exchange(modes, axis_index_groups=TEAMS)
        if repeat < STEPS - 1:
            send, fields = call(
                middle_kernel,
                both,
                [recv, fields, damping, inverse, cas, slope],
                flops=900_000_000,
                moved=3_000_000,
            )
    ends = call(
        last_kernel,
        f32(4, 72, TILE),
        [recv, fields, damping, cas],
        flops=200_000_000,
        moved=1_500_000,
    )
    ends = exchange(ends, axis_index_groups=PEERS)
    tangent = lax.ppermute(ends[:, 36:72], "seg", ring)
    base = lax.ppermute(ends[:, 0:36], "seg", ring)
    image, partial = call(
        dots_kernel,
        [f32(CUT, PLANES, NX), f32(16, 8, TILE)],
        [tangent, kry_f, gram],
        [pltpu.VMEM((TILE, TILE), jnp.float32)],
        flops=1_000_000,
        moved=1_300_000,
    )
    sums = everywhere(partial, axis_index_groups=columns)
    sums = jnp.sum(sums, axis=0)
    sums, base = lax.optimization_barrier((sums, base))
    sums = jnp.broadcast_to(sums[None], (2 * segs, 8, TILE))
    sums = everywhere(sums, axis_index_groups=planes)
    residual, vector, hess = call(
        finish_kernel,
        [f32(CUT, PLANES, NX)] * 2 + [f32(KRY + 1)],
        [sums, kry_f, image, state_f, base],
        flops=1_000_000,
        moved=1_500_000,
        keep=False,
    )
    return (residual.transpose(1, 0, 2), vector.transpose(1, 0, 2), hess)


def solution(mesh):
    return jax.shard_map(
        body,
        mesh=mesh,
        in_specs=(P("seg", "pen", None), P(None, "seg", "pen", None)),
        out_specs=(P("seg", "pen", None), P("seg", "pen", None), P()),
        check_vma=False,
    )
```

```python
import functools

import jax
import jax.numpy as jnp
import numpy as np
from jax import lax
from jax.experimental import pallas as pl
from jax.experimental.pallas import tpu as pltpu
from jax.sharding import PartitionSpec as P


NX = 384
NZ = 384
PLANES = 4
STEPS = 2
KRY = 16
SEGS = 16
PEN = 32
CUT = NZ // PEN
TEAM = 8
WIDE = NZ // TEAM
TILE = 128
INTERPRET = False

time_step = 0.0003
viscosity = 0.0226


def pen_index(y, team, member):
    return 16 * y + 4 * team + member


TEAMS = [[pen_index(y, q, r) for y in range(2) for r in range(4)] for q in range(4)]
PEERS = [[pen_index(y, q, r) for q in range(4)] for y in range(2) for r in range(4)]


def row_order():
    rows = []
    for y in range(2):
        for r in range(4):
            for q in range(4):
                rows += [CUT * pen_index(y, q, r) + n for n in range(CUT)]
    return np.array(rows)


def split_table(table):
    high = np.asarray(table, dtype=np.float32).astype(jnp.bfloat16)
    low = np.asarray(table - high.astype(np.float64), dtype=np.float32).astype(jnp.bfloat16)
    return np.concatenate([high, low], 0)


@functools.lru_cache(None)
def tables():
    count = NX
    k = np.arange(count)
    angle = 2.0 * np.pi * (np.outer(k, k) % count) / count
    cas = np.cos(angle) + np.sin(angle)
    signed = np.where(k <= count // 2, k, k - count)
    slopes = np.where(k == count // 2, 0, signed)
    slope = slopes[:, None] * (np.cos(angle) - np.sin(angle))
    order = row_order()
    pick = np.ix_(order, order)
    return (
        split_table(np.concatenate([cas, slope], 1)),
        split_table(cas[pick]),
        split_table(slope[pick].T),
    )


def halves(value):
    high = value.astype(jnp.bfloat16)
    low = (value - high.astype(jnp.float32)).astype(jnp.bfloat16)
    return high, low


def mm(a, b):
    return jnp.dot(a, b, preferred_element_type=jnp.float32)


def times_table(value, table_ref):
    high, low = halves(value)
    upper, lower = table_ref[0:NX, :], table_ref[NX : 2 * NX, :]
    left = jnp.concatenate([high, low, high], 1)
    return mm(left, jnp.concatenate([upper, upper, lower], 0))


def few_times_table(value, table_ref):
    high, low = halves(value)
    n = value.shape[0]
    both = mm(jnp.concatenate([high, low], 0), table_ref[0:NX, 0:NX])
    return both[0:n] + both[n : 2 * n] + mm(high, table_ref[NX : 2 * NX, 0:NX])


def table_times(table_ref, value):
    high, low = halves(value)
    upper, lower = table_ref[0:NX, :], table_ref[NX : 2 * NX, :]
    left = jnp.concatenate([upper, upper, lower], 1)
    return mm(left, jnp.concatenate([high, low, high], 0))


def call(kernel, outs, operands, scratch=(), flops=0, moved=0, keep=True):
    vmem = pl.BlockSpec(memory_space=pltpu.VMEM)
    single = not isinstance(outs, (list, tuple))
    shapes = [outs] if single else list(outs)
    if not INTERPRET:
        operands = [pltpu.with_memory_space_constraint(x, pltpu.VMEM) for x in operands]
        shapes = [pltpu.VMEM(x.shape, x.dtype) for x in shapes] if keep else shapes
    results = pl.pallas_call(
        kernel,
        in_specs=[vmem] * len(operands),
        out_specs=[vmem] * len(shapes),
        out_shape=shapes,
        scratch_shapes=list(scratch),
        cost_estimate=pl.CostEstimate(flops=flops, bytes_accessed=moved, transcendentals=0),
        compiler_params=pltpu.CompilerParams(vmem_limit_bytes=24 << 20),
        interpret=INTERPRET,
    )(*operands)
    return results[0] if single else results


def f32(*shape):
    return jax.ShapeDtypeStruct(shape, jnp.float32)


def tile(t):
    return slice(TILE * t, TILE * (t + 1))


def gather_rows(state_ref, last_ref, out_ref):
    for q in range(4):
        for member, ref in enumerate((state_ref, last_ref)):
            for t in range(3):
                row = 36 * member + CUT * t
                out_ref[q, row : row + CUT, :] = ref[:, q, tile(t)]


def spread(fields, inverse_ref, table_ref, send_ref):
    base, tangent = fields
    inverse = inverse_ref[...]
    spectra = jnp.concatenate([base * inverse, tangent * inverse, base, tangent], 0)
    both = times_table(spectra, table_ref)
    values, slopes = both[:, 0:NX], both[:, NX : 2 * NX]
    for m in range(TEAM):
        cut = slice(WIDE * m, WIDE * (m + 1))
        v = [values[WIDE * k : WIDE * (k + 1), cut] for k in range(4)]
        s = [slopes[WIDE * k : WIDE * (k + 1), cut] for k in range(4)]
        parts = [v[0], v[1], s[2][:, :32], v[2], v[3], s[2][:, 32:], s[3][:, :16]]
        block = jnp.concatenate(parts + [s[0], s[1], s[3][:, 16:]], 1)
        for t in range(3):
            send_ref[m, WIDE * t : WIDE * (t + 1), :] = block[:, tile(t)]


def first_kernel(recv_ref, inverse_ref, table_ref, send_ref, fields_ref):
    for q in range(4):
        for member in range(2):
            for t in range(3):
                row = 36 * member + CUT * t
                fields_ref[member, CUT * q : CUT * (q + 1), tile(t)] = recv_ref[
                    q, row : row + CUT, :
                ]
    spread((fields_ref[0], fields_ref[1]), inverse_ref, table_ref, send_ref)


def grid_kernel(recv_ref, cas_ref, slope_ref, send_ref):
    tiles = [
        jnp.concatenate([recv_ref[m, WIDE * t : WIDE * (t + 1), :] for m in range(TEAM)], 0)
        for t in range(3)
    ]
    tiles.append(jnp.concatenate([x[:, 96:] for x in (tiles[0], tiles[1], tiles[2], tiles[0])], 1))
    along_z = table_times(slope_ref, jnp.concatenate(tiles[0:2], 1))
    along_x = table_times(cas_ref, jnp.concatenate(tiles[2:4], 1))
    psi_z, vort_z = along_z[:, tile(0)], along_z[:, tile(1)]
    psi_x, vort_x = along_x[:, tile(0)], along_x[:, tile(1)]
    base = lax.broadcasted_iota(jnp.int32, (NZ, TILE), 1) < WIDE

    def moved(x):
        return pltpu.roll(x, WIDE, 1)

    first = psi_x * jnp.where(base, vort_z, moved(vort_z))
    first = first - psi_z * jnp.where(base, vort_x, moved(vort_x))
    second = moved(psi_x) * vort_z - moved(psi_z) * vort_x
    total = first + jnp.where(base, 0.0, second)
    modes = table_times(cas_ref, total)
    for m in range(TEAM):
        send_ref[m] = modes[WIDE * m : WIDE * (m + 1), :]


def advanced(recv_ref, fields_ref, damping_ref, table_ref):
    lines = [
        jnp.concatenate(
            [recv_ref[m, :, WIDE * member : WIDE * (member + 1)] for m in range(TEAM)], 1
        )
        for member in range(2)
    ]
    forcing = few_times_table(jnp.concatenate(lines, 0), table_ref)
    scale = time_step / (NX * NZ)
    damping = damping_ref[...]
    return [
        (fields_ref[member] + scale * forcing[WIDE * member : WIDE * (member + 1)]) * damping
        for member in range(2)
    ]


def middle_kernel(
    recv_ref, old_ref, damping_ref, inverse_ref, table_ref, send_ref, fields_ref
):
    fields = advanced(recv_ref, old_ref, damping_ref, table_ref)
    fields_ref[0] = fields[0]
    fields_ref[1] = fields[1]
    spread(fields, inverse_ref, table_ref, send_ref)


def last_kernel(recv_ref, old_ref, damping_ref, table_ref, out_ref):
    fields = advanced(recv_ref, old_ref, damping_ref, table_ref)
    for member in range(2):
        for q in range(4):
            for t in range(3):
                row = 36 * member + CUT * t
                out_ref[q, row : row + CUT, :] = fields[member][
                    CUT * q : CUT * (q + 1), tile(t)
                ]


def row_sums(value):
    ones = jnp.ones((8, TILE), jnp.bfloat16)
    first = value.astype(jnp.bfloat16)
    rest = value - first.astype(jnp.float32)
    second = rest.astype(jnp.bfloat16)
    third = (rest - second.astype(jnp.float32)).astype(jnp.bfloat16)
    dims = (((1,), (1,)), ((), ()))
    total = jnp.zeros((8, value.shape[0]), jnp.float32)
    for part in (third, second, first):
        total = total + lax.dot_general(ones, part, dims, preferred_element_type=jnp.float32)
    return total


def fold(value):
    return jnp.sum(value, axis=0, keepdims=True)


def fold(value):
    line = value[:, tile(0)] + value[:, tile(1)] + value[:, tile(2)]
    return jnp.sum(line, axis=0, keepdims=True)


def gram_kernel(kry_ref, out_ref, keep):
    for a in range(0, KRY, 4):
        for b in range(0, a + 1, 4):

            def step(g, sums):
                left = [kry_ref[a + i, g] for i in range(4)]
                right = [kry_ref[b + j, g] for j in range(4)]
                pairs = [(i, j) for i in range(4) for j in range(4)]
                return tuple(sums[4 * i + j] + left[i] * right[j] for i, j in pairs)

            zero = jnp.zeros((PLANES, NX), jnp.float32)
            sums = lax.fori_loop(0, CUT, step, (zero,) * 16)
            for i in range(4):
                for j in range(4):
                    line = fold(sums[4 * i + j])
                    keep[KRY * (a + i) + b + j : KRY * (a + i) + b + j + 1, :] = line
                    if a != b:
                        keep[KRY * (b + j) + a + i : KRY * (b + j) + a + i + 1, :] = line
    packed = row_sums(keep[...])
    row = lax.broadcasted_iota(jnp.int32, (8, TILE), 0)
    out_ref[...] = jnp.where(
        row == 1, packed[:, 0:TILE], jnp.where(row == 2, packed[:, TILE : 2 * TILE], 0.0)
    )


def place(planes_ref, out_ref):
    for p in range(PLANES):
        for t in range(3):
            out_ref[:, p, tile(t)] = planes_ref[p, CUT * t : CUT * (t + 1), :]


def dots_kernel(planes_ref, kry_ref, gram_ref, image_ref, out_ref, keep):
    place(planes_ref, image_ref)
    image = image_ref[...] - kry_ref[KRY - 1]
    image_ref[...] = image
    keep[...] = jnp.zeros_like(keep)
    for k in range(KRY):
        keep[k : k + 1, :] = fold(jnp.sum(kry_ref[k] * image, axis=0))
    keep[KRY : KRY + 1, :] = fold(jnp.sum(image * image, axis=0))
    packed = row_sums(keep[...])
    row = lax.broadcasted_iota(jnp.int32, (8, TILE), 0)
    sums = jnp.where(row == 0, packed, gram_ref[...])
    for m in range(out_ref.shape[0]):
        out_ref[m] = sums


def finish_kernel(
    sums_ref, kry_ref, image_ref, state_ref, planes_ref, residual_ref, next_ref, hess_ref
):
    place(planes_ref, residual_ref)
    residual_ref[...] = residual_ref[...] - state_ref[...]
    total = float(SEGS * PLANES * NZ * NX)
    sums = sums_ref[0]
    for s in range(1, sums_ref.shape[0]):
        sums = sums + sums_ref[s]
    sums = sums / total
    coeffs = [sums[0:1, k : k + 1] for k in range(KRY)]
    remain = image_ref[...]
    for k in range(KRY):
        remain = remain - coeffs[k] * kry_ref[k]
    lane = lax.broadcasted_iota(jnp.int32, (1, TILE), 1)
    inner = jnp.zeros((1, TILE), jnp.float32)
    outer = [inner, inner]
    for k in range(KRY):
        inner = jnp.where(lane % KRY == k, coeffs[k], inner)
        half, block = k // 8, k % 8
        outer[half] = jnp.where(lane // KRY == block, coeffs[k], outer[half])
    line = jnp.where(lane < KRY, sums[0:1] * sums[0:1], 0.0)
    quadratic = inner * (outer[0] * sums[1:2] + outer[1] * sums[2:3]) - 2.0 * line
    squared = sums[0:1, KRY : KRY + 1] + jnp.sum(quadratic, axis=1, keepdims=True)
    norm = jnp.sqrt(jnp.maximum(squared, 0.0) + 1e-06)
    next_ref[...] = remain / norm
    hess = jnp.where(lane == KRY, norm, sums[0:1])
    hess_ref[...] = hess[0, : KRY + 1]


def reduce_groups(segs):
    def number(place, inner):
        seg, y = place
        return seg * PEN + 16 * y + inner

    places = [(seg, y) for seg in range(segs) for y in range(2)]
    columns = [[number(place, inner) for inner in range(16)] for place in places]
    planes = [[number(place, inner) for place in places] for inner in range(16)]
    return columns, planes


def body(state, krylov):
    pen = lax.axis_index("pen")
    segs = lax.axis_size("seg")
    numbers = np.arange(NX)
    signed = np.where(numbers <= NX // 2, numbers, numbers - NX).astype(np.float32)
    steps = np.arange(WIDE)
    rows = CUT * (16 * (pen // 16) + pen % 4) + (4 * CUT * (steps // CUT) + steps % CUT)
    mode = jnp.where(rows <= NZ // 2, rows, rows - NZ).astype(jnp.float32)
    ksquare = mode[:, None] ** 2 + signed[None, :] ** 2
    inverse = jnp.where(ksquare > 0, 1.0 / jnp.where(ksquare > 0, ksquare, 1.0), 0.0)
    damping = 1.0 / (1.0 + time_step * viscosity * ksquare)
    table, cas_z, slope_z = [jnp.asarray(t) for t in tables()]
    state_f = state.transpose(1, 0, 2)
    kry_f = krylov.transpose(0, 2, 1, 3)
    exchange = functools.partial(
        lax.all_to_all, axis_name="pen", split_axis=0, concat_axis=0, tiled=True
    )
    everywhere = functools.partial(
        lax.all_to_all, axis_name=("seg", "pen"), split_axis=0, concat_axis=0, tiled=True
    )
    columns, planes = reduce_groups(segs)
    ring = [(s, (s + 1) % segs) for s in range(segs)]

    whole = pl.BlockSpec((CUT, PLANES, NX), lambda i: (0, 0, 0))
    last = pl.BlockSpec((None, CUT, PLANES, NX), lambda i: (KRY - 1, 0, 0, 0))
    inputs = [state_f, kry_f]
    if not INTERPRET:
        inputs = [pltpu.with_memory_space_constraint(x, pltpu.HBM) for x in inputs]
    packed = pl.pallas_call(
        gather_rows,
        grid=(1,),
        in_specs=[whole, last],
        out_specs=pl.BlockSpec((4, 72, TILE), lambda i: (0, 0, 0)),
        out_shape=f32(4, 72, TILE),
        compiler_params=pltpu.CompilerParams(vmem_limit_bytes=24 << 20),
        interpret=INTERPRET,
    )(*inputs)
    packed = exchange(packed, axis_index_groups=PEERS)
    both = (f32(TEAM, 144, TILE), f32(2, WIDE, NX))
    send, fields = call(
        first_kernel, both, [packed, inverse, table], flops=700_000_000, moved=3_000_000
    )
    for repeat in range(STEPS):
        recv = exchange(send, axis_index_groups=TEAMS)
        modes = call(
            grid_kernel,
            f32(TEAM, WIDE, TILE),
            [recv, cas_z, slope_z],
            flops=900_000_000,
            moved=2_500_000,
        )
        recv = exchange(modes, axis_index_groups=TEAMS)
        if repeat < STEPS - 1:
            send, fields = call(
                middle_kernel,
                both,
                [recv, fields, damping, inverse, table],
                flops=900_000_000,
                moved=3_000_000,
            )
    ends = call(
        last_kernel,
        f32(4, 72, TILE),
        [recv, fields, damping, table],
        flops=200_000_000,
        moved=1_500_000,
    )
    ends = exchange(ends, axis_index_groups=PEERS)
    tangent = lax.ppermute(ends[:, 36:72], "seg", ring)
    gram = call(
        gram_kernel,
        f32(8, TILE),
        [kry_f],
        [pltpu.VMEM((KRY * KRY, TILE), jnp.float32)],
        flops=10_000_000,
        moved=1_300_000,
    )
    base, gram = lax.optimization_barrier((ends[:, 0:36], gram))
    base = lax.ppermute(base, "seg", ring)
    image, partial = call(
        dots_kernel,
        [f32(CUT, PLANES, NX), f32(16, 8, TILE)],
        [tangent, kry_f, gram],
        [pltpu.VMEM((TILE, TILE), jnp.float32)],
        flops=1_000_000,
        moved=1_300_000,
    )
    sums = everywhere(partial, axis_index_groups=columns)
    sums = jnp.sum(sums, axis=0)
    sums, base = lax.optimization_barrier((sums, base))
    sums = jnp.broadcast_to(sums[None], (2 * segs, 8, TILE))
    sums = everywhere(sums, axis_index_groups=planes)
    residual, vector, hess = call(
        finish_kernel,
        [f32(CUT, PLANES, NX)] * 2 + [f32(KRY + 1)],
        [sums, kry_f, image, state_f, base],
        flops=1_000_000,
        moved=1_500_000,
        keep=False,
    )
    return (residual.transpose(1, 0, 2), vector.transpose(1, 0, 2), hess)


def solution(mesh):
    return jax.shard_map(
        body,
        mesh=mesh,
        in_specs=(P("seg", "pen", None), P(None, "seg", "pen", None)),
        out_specs=(P("seg", "pen", None), P("seg", "pen", None), P()),
        check_vma=False,
    )
```

```python
import functools

import jax
import jax.numpy as jnp
import numpy as np
from jax import lax
from jax.experimental import pallas as pl
from jax.experimental.pallas import tpu as pltpu
from jax.sharding import PartitionSpec as P


NX = 384
NZ = 384
PLANES = 4
STEPS = 2
KRY = 16
SEGS = 16
PEN = 32
CUT = NZ // PEN
TEAM = 8
WIDE = NZ // TEAM
TILE = 128
INTERPRET = False

time_step = 0.0003
viscosity = 0.0226


def pen_index(y, team, member):
    return 16 * y + 4 * team + member


TEAMS = [[pen_index(y, q, r) for y in range(2) for r in range(4)] for q in range(4)]
PEERS = [[pen_index(y, q, r) for q in range(4)] for y in range(2) for r in range(4)]


def row_order():
    rows = []
    for y in range(2):
        for r in range(4):
            for q in range(4):
                rows += [CUT * pen_index(y, q, r) + n for n in range(CUT)]
    return np.array(rows)


def split_table(table):
    high = np.asarray(table, dtype=np.float32).astype(jnp.bfloat16)
    low = np.asarray(table - high.astype(np.float64), dtype=np.float32).astype(jnp.bfloat16)
    return np.concatenate([high, low], 0)


@functools.lru_cache(None)
def tables():
    count = NX
    k = np.arange(count)
    angle = 2.0 * np.pi * (np.outer(k, k) % count) / count
    cas = np.cos(angle) + np.sin(angle)
    signed = np.where(k <= count // 2, k, k - count)
    slopes = np.where(k == count // 2, 0, signed)
    slope = slopes[:, None] * (np.cos(angle) - np.sin(angle))
    order = row_order()
    pick = np.ix_(order, order)
    return (
        split_table(np.concatenate([cas, slope], 1)),
        split_table(cas[pick]),
        split_table(slope[pick].T),
    )


def halves(value):
    high = value.astype(jnp.bfloat16)
    low = (value - high.astype(jnp.float32)).astype(jnp.bfloat16)
    return high, low


def mm(a, b):
    return jnp.dot(a, b, preferred_element_type=jnp.float32)


def times_table(value, table_ref):
    high, low = halves(value)
    upper, lower = table_ref[0:NX, :], table_ref[NX : 2 * NX, :]
    left = jnp.concatenate([high, low, high], 1)
    return mm(left, jnp.concatenate([upper, upper, lower], 0))


def few_times_table(value, table_ref):
    high, low = halves(value)
    n = value.shape[0]
    both = mm(jnp.concatenate([high, low], 0), table_ref[0:NX, 0:NX])
    return both[0:n] + both[n : 2 * n] + mm(high, table_ref[NX : 2 * NX, 0:NX])


def table_times(table_ref, value):
    high, low = halves(value)
    upper, lower = table_ref[0:NX, :], table_ref[NX : 2 * NX, :]
    left = jnp.concatenate([upper, upper, lower], 1)
    return mm(left, jnp.concatenate([high, low, high], 0))


def call(kernel, outs, operands, scratch=(), flops=0, moved=0, keep=True):
    vmem = pl.BlockSpec(memory_space=pltpu.VMEM)
    single = not isinstance(outs, (list, tuple))
    shapes = [outs] if single else list(outs)
    if not INTERPRET:
        operands = [pltpu.with_memory_space_constraint(x, pltpu.VMEM) for x in operands]
        shapes = [pltpu.VMEM(x.shape, x.dtype) for x in shapes] if keep else shapes
    results = pl.pallas_call(
        kernel,
        in_specs=[vmem] * len(operands),
        out_specs=[vmem] * len(shapes),
        out_shape=shapes,
        scratch_shapes=list(scratch),
        cost_estimate=pl.CostEstimate(flops=flops, bytes_accessed=moved, transcendentals=0),
        compiler_params=pltpu.CompilerParams(vmem_limit_bytes=24 << 20),
        interpret=INTERPRET,
    )(*operands)
    return results[0] if single else results


def f32(*shape):
    return jax.ShapeDtypeStruct(shape, jnp.float32)


def tile(t):
    return slice(TILE * t, TILE * (t + 1))


def gather_rows(state_ref, last_ref, out_ref):
    for q in range(4):
        for member, ref in enumerate((state_ref, last_ref)):
            for t in range(3):
                row = 36 * member + CUT * t
                out_ref[q, row : row + CUT, :] = ref[:, q, tile(t)]


def spread(fields, inverse_ref, table_ref, send_ref):
    base, tangent = fields
    inverse = inverse_ref[...]
    spectra = jnp.concatenate([base * inverse, tangent * inverse, base, tangent], 0)
    both = times_table(spectra, table_ref)
    values, slopes = both[:, 0:NX], both[:, NX : 2 * NX]
    for m in range(TEAM):
        cut = slice(WIDE * m, WIDE * (m + 1))
        v = [values[WIDE * k : WIDE * (k + 1), cut] for k in range(4)]
        s = [slopes[WIDE * k : WIDE * (k + 1), cut] for k in range(4)]
        parts = [v[0], v[1], s[2][:, :32], v[2], v[3], s[2][:, 32:], s[3][:, :16]]
        block = jnp.concatenate(parts + [s[0], s[1], s[3][:, 16:]], 1)
        for t in range(3):
            send_ref[m, WIDE * t : WIDE * (t + 1), :] = block[:, tile(t)]


def first_kernel(recv_ref, inverse_ref, table_ref, send_ref, fields_ref):
    for q in range(4):
        for member in range(2):
            for t in range(3):
                row = 36 * member + CUT * t
                fields_ref[member, CUT * q : CUT * (q + 1), tile(t)] = recv_ref[
                    q, row : row + CUT, :
                ]
    spread((fields_ref[0], fields_ref[1]), inverse_ref, table_ref, send_ref)


def grid_kernel(recv_ref, cas_ref, slope_ref, send_ref):
    tiles = [
        jnp.concatenate([recv_ref[m, WIDE * t : WIDE * (t + 1), :] for m in range(TEAM)], 0)
        for t in range(3)
    ]
    tiles.append(jnp.concatenate([x[:, 96:] for x in (tiles[0], tiles[1], tiles[2], tiles[0])], 1))
    along_z = table_times(slope_ref, jnp.concatenate(tiles[0:2], 1))
    along_x = table_times(cas_ref, jnp.concatenate(tiles[2:4], 1))
    psi_z, vort_z = along_z[:, tile(0)], along_z[:, tile(1)]
    psi_x, vort_x = along_x[:, tile(0)], along_x[:, tile(1)]
    base = lax.broadcasted_iota(jnp.int32, (NZ, TILE), 1) < WIDE

    def moved(x):
        return pltpu.roll(x, WIDE, 1)

    first = psi_x * jnp.where(base, vort_z, moved(vort_z))
    first = first - psi_z * jnp.where(base, vort_x, moved(vort_x))
    second = moved(psi_x) * vort_z - moved(psi_z) * vort_x
    total = first + jnp.where(base, 0.0, second)
    modes = table_times(cas_ref, total)
    for m in range(TEAM):
        send_ref[m] = modes[WIDE * m : WIDE * (m + 1), :]


def advanced(recv_ref, fields_ref, damping_ref, table_ref):
    lines = [
        jnp.concatenate(
            [recv_ref[m, :, WIDE * member : WIDE * (member + 1)] for m in range(TEAM)], 1
        )
        for member in range(2)
    ]
    forcing = few_times_table(jnp.concatenate(lines, 0), table_ref)
    scale = time_step / (NX * NZ)
    damping = damping_ref[...]
    return [
        (fields_ref[member] + scale * forcing[WIDE * member : WIDE * (member + 1)]) * damping
        for member in range(2)
    ]


def middle_kernel(
    recv_ref, old_ref, damping_ref, inverse_ref, table_ref, send_ref, fields_ref
):
    fields = advanced(recv_ref, old_ref, damping_ref, table_ref)
    fields_ref[0] = fields[0]
    fields_ref[1] = fields[1]
    spread(fields, inverse_ref, table_ref, send_ref)


def last_kernel(recv_ref, old_ref, damping_ref, table_ref, out_ref):
    fields = advanced(recv_ref, old_ref, damping_ref, table_ref)
    for member in range(2):
        for q in range(4):
            for t in range(3):
                row = 36 * member + CUT * t
                out_ref[q, row : row + CUT, :] = fields[member][
                    CUT * q : CUT * (q + 1), tile(t)
                ]


def row_sums(value):
    ones = jnp.ones((8, TILE), jnp.bfloat16)
    first = value.astype(jnp.bfloat16)
    rest = value - first.astype(jnp.float32)
    second = rest.astype(jnp.bfloat16)
    third = (rest - second.astype(jnp.float32)).astype(jnp.bfloat16)
    dims = (((1,), (1,)), ((), ()))
    total = jnp.zeros((8, value.shape[0]), jnp.float32)
    for part in (third, second, first):
        total = total + lax.dot_general(ones, part, dims, preferred_element_type=jnp.float32)
    return total


def fold(value):
    return jnp.sum(value, axis=0, keepdims=True)


def fold(value):
    line = value[:, tile(0)] + value[:, tile(1)] + value[:, tile(2)]
    return jnp.sum(line, axis=0, keepdims=True)


def gram_kernel(kry_ref, out_ref, keep):
    for a in range(0, KRY, 4):
        for b in range(0, a + 1, 4):

            def step(g, sums):
                left = [kry_ref[a + i, g] for i in range(4)]
                right = [kry_ref[b + j, g] for j in range(4)]
                pairs = [(i, j) for i in range(4) for j in range(4)]
                return tuple(sums[4 * i + j] + left[i] * right[j] for i, j in pairs)

            zero = jnp.zeros((PLANES, NX), jnp.float32)
            sums = lax.fori_loop(0, CUT, step, (zero,) * 16)
            for i in range(4):
                for j in range(4):
                    line = fold(sums[4 * i + j])
                    keep[KRY * (a + i) + b + j : KRY * (a + i) + b + j + 1, :] = line
                    if a != b:
                        keep[KRY * (b + j) + a + i : KRY * (b + j) + a + i + 1, :] = line
    packed = row_sums(keep[...])
    row = lax.broadcasted_iota(jnp.int32, (8, TILE), 0)
    out_ref[...] = jnp.where(
        row == 1, packed[:, 0:TILE], jnp.where(row == 2, packed[:, TILE : 2 * TILE], 0.0)
    )


def place(planes_ref, out_ref):
    for p in range(PLANES):
        for t in range(3):
            row = 36 * p + CUT * t
            out_ref[:, p, tile(t)] = planes_ref[row : row + CUT, :]


def dots_kernel(planes_ref, kry_ref, gram_ref, image_ref, out_ref, keep):
    place(planes_ref, image_ref)
    image = image_ref[...] - kry_ref[KRY - 1]
    image_ref[...] = image
    keep[...] = jnp.zeros_like(keep)
    for k in range(KRY):
        keep[k : k + 1, :] = fold(jnp.sum(kry_ref[k] * image, axis=0))
    keep[KRY : KRY + 1, :] = fold(jnp.sum(image * image, axis=0))
    packed = row_sums(keep[...])
    row = lax.broadcasted_iota(jnp.int32, (8, TILE), 0)
    sums = jnp.where(row == 0, packed, gram_ref[...])
    for m in range(out_ref.shape[0]):
        out_ref[m] = sums


def finish_kernel(
    sums_ref, kry_ref, image_ref, state_ref, planes_ref, residual_ref, next_ref, hess_ref
):
    place(planes_ref, residual_ref)
    residual_ref[...] = residual_ref[...] - state_ref[...]
    total = float(SEGS * PLANES * NZ * NX)
    sums = sums_ref[0]
    for s in range(1, sums_ref.shape[0]):
        sums = sums + sums_ref[s]
    sums = sums / total
    coeffs = [sums[0:1, k : k + 1] for k in range(KRY)]
    remain = image_ref[...]
    for k in range(KRY):
        remain = remain - coeffs[k] * kry_ref[k]
    lane = lax.broadcasted_iota(jnp.int32, (1, TILE), 1)
    inner = jnp.zeros((1, TILE), jnp.float32)
    outer = [inner, inner]
    for k in range(KRY):
        inner = jnp.where(lane % KRY == k, coeffs[k], inner)
        half, block = k // 8, k % 8
        outer[half] = jnp.where(lane // KRY == block, coeffs[k], outer[half])
    line = jnp.where(lane < KRY, sums[0:1] * sums[0:1], 0.0)
    quadratic = inner * (outer[0] * sums[1:2] + outer[1] * sums[2:3]) - 2.0 * line
    squared = sums[0:1, KRY : KRY + 1] + jnp.sum(quadratic, axis=1, keepdims=True)
    norm = jnp.sqrt(jnp.maximum(squared, 0.0) + 1e-06)
    next_ref[...] = remain / norm
    hess = jnp.where(lane == KRY, norm, sums[0:1])
    hess_ref[...] = hess[0, : KRY + 1]


def reduce_groups(segs):
    def number(place, inner):
        seg, y = place
        return seg * PEN + 16 * y + inner

    places = [(seg, y) for seg in range(segs) for y in range(2)]
    columns = [[number(place, inner) for inner in range(16)] for place in places]
    planes = [[number(place, inner) for place in places] for inner in range(16)]
    return columns, planes


def body(state, krylov):
    pen = lax.axis_index("pen")
    segs = lax.axis_size("seg")
    numbers = np.arange(NX)
    signed = np.where(numbers <= NX // 2, numbers, numbers - NX).astype(np.float32)
    steps = np.arange(WIDE)
    rows = CUT * (16 * (pen // 16) + pen % 4) + (4 * CUT * (steps // CUT) + steps % CUT)
    mode = jnp.where(rows <= NZ // 2, rows, rows - NZ).astype(jnp.float32)
    ksquare = mode[:, None] ** 2 + signed[None, :] ** 2
    inverse = jnp.where(ksquare > 0, 1.0 / jnp.where(ksquare > 0, ksquare, 1.0), 0.0)
    damping = 1.0 / (1.0 + time_step * viscosity * ksquare)
    table, cas_z, slope_z = [jnp.asarray(t) for t in tables()]
    state_f = state.transpose(1, 0, 2)
    kry_f = krylov.transpose(0, 2, 1, 3)
    exchange = functools.partial(
        lax.all_to_all, axis_name="pen", split_axis=0, concat_axis=0, tiled=True
    )
    everywhere = functools.partial(
        lax.all_to_all, axis_name=("seg", "pen"), split_axis=0, concat_axis=0, tiled=True
    )
    columns, planes = reduce_groups(segs)
    ring = [(s, (s + 1) % segs) for s in range(segs)]

    whole = pl.BlockSpec((CUT, PLANES, NX), lambda i: (0, 0, 0))
    last = pl.BlockSpec((None, CUT, PLANES, NX), lambda i: (KRY - 1, 0, 0, 0))
    inputs = [state_f, kry_f]
    if not INTERPRET:
        inputs = [pltpu.with_memory_space_constraint(x, pltpu.HBM) for x in inputs]
    packed = pl.pallas_call(
        gather_rows,
        grid=(1,),
        in_specs=[whole, last],
        out_specs=pl.BlockSpec((4, 72, TILE), lambda i: (0, 0, 0)),
        out_shape=f32(4, 72, TILE),
        compiler_params=pltpu.CompilerParams(vmem_limit_bytes=24 << 20),
        interpret=INTERPRET,
    )(*inputs)
    packed = exchange(packed, axis_index_groups=PEERS)
    both = (f32(TEAM, 144, TILE), f32(2, WIDE, NX))
    send, fields = call(
        first_kernel, both, [packed, inverse, table], flops=700_000_000, moved=3_000_000
    )
    for repeat in range(STEPS):
        recv = exchange(send, axis_index_groups=TEAMS)
        modes = call(
            grid_kernel,
            f32(TEAM, WIDE, TILE),
            [recv, cas_z, slope_z],
            flops=900_000_000,
            moved=2_500_000,
        )
        recv = exchange(modes, axis_index_groups=TEAMS)
        if repeat < STEPS - 1:
            send, fields = call(
                middle_kernel,
                both,
                [recv, fields, damping, inverse, table],
                flops=900_000_000,
                moved=3_000_000,
            )
    ends = call(
        last_kernel,
        f32(4, 72, TILE),
        [recv, fields, damping, table],
        flops=200_000_000,
        moved=1_500_000,
    )
    ends = exchange(ends, axis_index_groups=PEERS)
    tangent = lax.ppermute(ends[:, 36:72].reshape(144, TILE), "seg", ring)
    gram = call(
        gram_kernel,
        f32(8, TILE),
        [kry_f],
        [pltpu.VMEM((KRY * KRY, TILE), jnp.float32)],
        flops=10_000_000,
        moved=1_300_000,
    )
    base, gram = lax.optimization_barrier((ends[:, 0:36].reshape(144, TILE), gram))
    base = lax.ppermute(base, "seg", ring)
    image, partial = call(
        dots_kernel,
        [f32(CUT, PLANES, NX), f32(16, 8, TILE)],
        [tangent, kry_f, gram],
        [pltpu.VMEM((TILE, TILE), jnp.float32)],
        flops=1_000_000,
        moved=1_300_000,
    )
    sums = everywhere(partial, axis_index_groups=columns)
    sums = jnp.sum(sums, axis=0)
    sums, base = lax.optimization_barrier((sums, base))
    sums = jnp.broadcast_to(sums[None], (2 * segs, 8, TILE))
    sums = everywhere(sums, axis_index_groups=planes)
    residual, vector, hess = call(
        finish_kernel,
        [f32(CUT, PLANES, NX)] * 2 + [f32(KRY + 1)],
        [sums, kry_f, image, state_f, base],
        flops=1_000_000,
        moved=1_500_000,
        keep=False,
    )
    return (residual.transpose(1, 0, 2), vector.transpose(1, 0, 2), hess)


def solution(mesh):
    return jax.shard_map(
        body,
        mesh=mesh,
        in_specs=(P("seg", "pen", None), P(None, "seg", "pen", None)),
        out_specs=(P("seg", "pen", None), P("seg", "pen", None), P()),
        check_vma=False,
    )
```

```python
import functools

import jax
import jax.numpy as jnp
import numpy as np
from jax import lax
from jax.experimental import pallas as pl
from jax.experimental.pallas import tpu as pltpu
from jax.sharding import PartitionSpec as P


NX = 384
NZ = 384
PLANES = 4
STEPS = 2
KRY = 16
SEGS = 16
PEN = 32
CUT = NZ // PEN
TEAM = 8
WIDE = NZ // TEAM
TILE = 128
INTERPRET = False

time_step = 0.0003
viscosity = 0.0226


def pen_index(y, team, member):
    return 16 * y + 4 * team + member


TEAMS = [[pen_index(y, q, r) for y in range(2) for r in range(4)] for q in range(4)]
PEERS = [[pen_index(y, q, r) for q in range(4)] for y in range(2) for r in range(4)]


def row_order():
    rows = []
    for y in range(2):
        for r in range(4):
            for q in range(4):
                rows += [CUT * pen_index(y, q, r) + n for n in range(CUT)]
    return np.array(rows)


def split_table(table):
    high = np.asarray(table, dtype=np.float32).astype(jnp.bfloat16)
    low = np.asarray(table - high.astype(np.float64), dtype=np.float32).astype(jnp.bfloat16)
    return np.concatenate([high, low], 0)


@functools.lru_cache(None)
def tables():
    count = NX
    k = np.arange(count)
    angle = 2.0 * np.pi * (np.outer(k, k) % count) / count
    cas = np.cos(angle) + np.sin(angle)
    signed = np.where(k <= count // 2, k, k - count)
    slopes = np.where(k == count // 2, 0, signed)
    slope = slopes[:, None] * (np.cos(angle) - np.sin(angle))
    order = row_order()
    pick = np.ix_(order, order)
    return (
        split_table(np.concatenate([cas, slope], 1)),
        split_table(cas[pick]),
        split_table(slope[pick].T),
    )


def halves(value):
    high = value.astype(jnp.bfloat16)
    low = (value - high.astype(jnp.float32)).astype(jnp.bfloat16)
    return high, low


def mm(a, b):
    return jnp.dot(a, b, preferred_element_type=jnp.float32)


def times_table(value, table_ref):
    high, low = halves(value)
    upper, lower = table_ref[0:NX, :], table_ref[NX : 2 * NX, :]
    left = jnp.concatenate([high, low, high], 1)
    return mm(left, jnp.concatenate([upper, upper, lower], 0))


def few_times_table(value, table_ref):
    high, low = halves(value)
    n = value.shape[0]
    both = mm(jnp.concatenate([high, low], 0), table_ref[0:NX, 0:NX])
    return both[0:n] + both[n : 2 * n] + mm(high, table_ref[NX : 2 * NX, 0:NX])


def table_times(table_ref, value):
    high, low = halves(value)
    upper, lower = table_ref[0:NX, :], table_ref[NX : 2 * NX, :]
    left = jnp.concatenate([upper, upper, lower], 1)
    return mm(left, jnp.concatenate([high, low, high], 0))


def call(kernel, outs, operands, scratch=(), flops=0, moved=0, keep=True):
    vmem = pl.BlockSpec(memory_space=pltpu.VMEM)
    single = not isinstance(outs, (list, tuple))
    shapes = [outs] if single else list(outs)
    if not INTERPRET:
        operands = [pltpu.with_memory_space_constraint(x, pltpu.VMEM) for x in operands]
        shapes = [pltpu.VMEM(x.shape, x.dtype) for x in shapes] if keep else shapes
    results = pl.pallas_call(
        kernel,
        in_specs=[vmem] * len(operands),
        out_specs=[vmem] * len(shapes),
        out_shape=shapes,
        scratch_shapes=list(scratch),
        cost_estimate=pl.CostEstimate(flops=flops, bytes_accessed=moved, transcendentals=0),
        compiler_params=pltpu.CompilerParams(vmem_limit_bytes=24 << 20),
        interpret=INTERPRET,
    )(*operands)
    return results[0] if single else results


def f32(*shape):
    return jax.ShapeDtypeStruct(shape, jnp.float32)


def tile(t):
    return slice(TILE * t, TILE * (t + 1))


def gather_rows(state_ref, kry_ref, out_ref, state_rows, last_rows, arrived):
    copies = [
        pltpu.make_async_copy(state_ref, state_rows, arrived.at[0]),
        pltpu.make_async_copy(kry_ref.at[KRY - 1], last_rows, arrived.at[1]),
    ]
    for copy in copies:
        copy.start()
    for member, rows in enumerate((state_rows, last_rows)):
        copies[member].wait()
        for q in range(4):
            for t in range(3):
                row = 36 * member + CUT * t
                out_ref[q, row : row + CUT, :] = rows[:, q, tile(t)]


def spread(fields, inverse_ref, table_ref, send_ref):
    base, tangent = fields
    inverse = inverse_ref[...]
    spectra = jnp.concatenate([base * inverse, tangent * inverse, base, tangent], 0)
    both = times_table(spectra, table_ref)
    values, slopes = both[:, 0:NX], both[:, NX : 2 * NX]
    for m in range(TEAM):
        cut = slice(WIDE * m, WIDE * (m + 1))
        v = [values[WIDE * k : WIDE * (k + 1), cut] for k in range(4)]
        s = [slopes[WIDE * k : WIDE * (k + 1), cut] for k in range(4)]
        parts = [v[0], v[1], s[2][:, :32], v[2], v[3], s[2][:, 32:], s[3][:, :16]]
        block = jnp.concatenate(parts + [s[0], s[1], s[3][:, 16:]], 1)
        for t in range(3):
            send_ref[m, WIDE * t : WIDE * (t + 1), :] = block[:, tile(t)]


def first_kernel(recv_ref, inverse_ref, table_ref, send_ref, fields_ref):
    for q in range(4):
        for member in range(2):
            for t in range(3):
                row = 36 * member + CUT * t
                fields_ref[member, CUT * q : CUT * (q + 1), tile(t)] = recv_ref[
                    q, row : row + CUT, :
                ]
    spread((fields_ref[0], fields_ref[1]), inverse_ref, table_ref, send_ref)


def grid_kernel(recv_ref, cas_ref, slope_ref, send_ref):
    tiles = [
        jnp.concatenate([recv_ref[m, WIDE * t : WIDE * (t + 1), :] for m in range(TEAM)], 0)
        for t in range(3)
    ]
    tiles.append(jnp.concatenate([x[:, 96:] for x in (tiles[0], tiles[1], tiles[2], tiles[0])], 1))
    along_z = table_times(slope_ref, jnp.concatenate(tiles[0:2], 1))
    along_x = table_times(cas_ref, jnp.concatenate(tiles[2:4], 1))
    psi_z, vort_z = along_z[:, tile(0)], along_z[:, tile(1)]
    psi_x, vort_x = along_x[:, tile(0)], along_x[:, tile(1)]
    base = lax.broadcasted_iota(jnp.int32, (NZ, TILE), 1) < WIDE

    def moved(x):
        return pltpu.roll(x, WIDE, 1)

    first = psi_x * jnp.where(base, vort_z, moved(vort_z))
    first = first - psi_z * jnp.where(base, vort_x, moved(vort_x))
    second = moved(psi_x) * vort_z - moved(psi_z) * vort_x
    total = first + jnp.where(base, 0.0, second)
    modes = table_times(cas_ref, total)
    for m in range(TEAM):
        send_ref[m] = modes[WIDE * m : WIDE * (m + 1), :]


def advanced(recv_ref, fields_ref, damping_ref, table_ref):
    lines = [
        jnp.concatenate(
            [recv_ref[m, :, WIDE * member : WIDE * (member + 1)] for m in range(TEAM)], 1
        )
        for member in range(2)
    ]
    forcing = few_times_table(jnp.concatenate(lines, 0), table_ref)
    scale = time_step / (NX * NZ)
    damping = damping_ref[...]
    return [
        (fields_ref[member] + scale * forcing[WIDE * member : WIDE * (member + 1)]) * damping
        for member in range(2)
    ]


def middle_kernel(
    recv_ref, old_ref, damping_ref, inverse_ref, table_ref, send_ref, fields_ref
):
    fields = advanced(recv_ref, old_ref, damping_ref, table_ref)
    fields_ref[0] = fields[0]
    fields_ref[1] = fields[1]
    spread(fields, inverse_ref, table_ref, send_ref)


def last_kernel(recv_ref, old_ref, damping_ref, table_ref, out_ref):
    fields = advanced(recv_ref, old_ref, damping_ref, table_ref)
    for member in range(2):
        for q in range(4):
            for t in range(3):
                row = 36 * member + CUT * t
                out_ref[q, row : row + CUT, :] = fields[member][
                    CUT * q : CUT * (q + 1), tile(t)
                ]


def row_sums(value):
    ones = jnp.ones((8, TILE), jnp.bfloat16)
    first = value.astype(jnp.bfloat16)
    rest = value - first.astype(jnp.float32)
    second = rest.astype(jnp.bfloat16)
    third = (rest - second.astype(jnp.float32)).astype(jnp.bfloat16)
    dims = (((1,), (1,)), ((), ()))
    total = jnp.zeros((8, value.shape[0]), jnp.float32)
    for part in (third, second, first):
        total = total + lax.dot_general(ones, part, dims, preferred_element_type=jnp.float32)
    return total


def fold(value):
    return jnp.sum(value, axis=0, keepdims=True)


def fold(value):
    line = value[:, tile(0)] + value[:, tile(1)] + value[:, tile(2)]
    return jnp.sum(line, axis=0, keepdims=True)


def gram_kernel(kry_ref, out_ref, keep):
    for a in range(0, KRY, 4):
        for b in range(0, a + 1, 4):

            def step(g, sums):
                left = [kry_ref[a + i, g] for i in range(4)]
                right = [kry_ref[b + j, g] for j in range(4)]
                pairs = [(i, j) for i in range(4) for j in range(4)]
                return tuple(sums[4 * i + j] + left[i] * right[j] for i, j in pairs)

            zero = jnp.zeros((PLANES, NX), jnp.float32)
            sums = lax.fori_loop(0, CUT, step, (zero,) * 16)
            for i in range(4):
                for j in range(4):
                    line = fold(sums[4 * i + j])
                    keep[KRY * (a + i) + b + j : KRY * (a + i) + b + j + 1, :] = line
                    if a != b:
                        keep[KRY * (b + j) + a + i : KRY * (b + j) + a + i + 1, :] = line
    packed = row_sums(keep[...])
    row = lax.broadcasted_iota(jnp.int32, (8, TILE), 0)
    out_ref[...] = jnp.where(
        row == 1, packed[:, 0:TILE], jnp.where(row == 2, packed[:, TILE : 2 * TILE], 0.0)
    )


def place(planes_ref, out_ref):
    for p in range(PLANES):
        for t in range(3):
            row = 36 * p + CUT * t
            out_ref[:, p, tile(t)] = planes_ref[row : row + CUT, :]


def dots_kernel(planes_ref, kry_ref, gram_ref, image_ref, out_ref, keep):
    place(planes_ref, image_ref)
    image = image_ref[...] - kry_ref[KRY - 1]
    image_ref[...] = image
    keep[...] = jnp.zeros_like(keep)
    for k in range(KRY):
        keep[k : k + 1, :] = fold(jnp.sum(kry_ref[k] * image, axis=0))
    keep[KRY : KRY + 1, :] = fold(jnp.sum(image * image, axis=0))
    packed = row_sums(keep[...])
    row = lax.broadcasted_iota(jnp.int32, (8, TILE), 0)
    sums = jnp.where(row == 0, packed, gram_ref[...])
    for m in range(out_ref.shape[0]):
        out_ref[m] = sums


def finish_kernel(
    sums_ref, kry_ref, image_ref, state_ref, planes_ref, residual_ref, next_ref, hess_ref
):
    place(planes_ref, residual_ref)
    residual_ref[...] = residual_ref[...] - state_ref[...]
    total = float(SEGS * PLANES * NZ * NX)
    sums = sums_ref[0]
    for s in range(1, sums_ref.shape[0]):
        sums = sums + sums_ref[s]
    sums = sums / total
    coeffs = [sums[0:1, k : k + 1] for k in range(KRY)]
    remain = image_ref[...]
    for k in range(KRY):
        remain = remain - coeffs[k] * kry_ref[k]
    lane = lax.broadcasted_iota(jnp.int32, (1, TILE), 1)
    inner = jnp.zeros((1, TILE), jnp.float32)
    outer = [inner, inner]
    for k in range(KRY):
        inner = jnp.where(lane % KRY == k, coeffs[k], inner)
        half, block = k // 8, k % 8
        outer[half] = jnp.where(lane // KRY == block, coeffs[k], outer[half])
    line = jnp.where(lane < KRY, sums[0:1] * sums[0:1], 0.0)
    quadratic = inner * (outer[0] * sums[1:2] + outer[1] * sums[2:3]) - 2.0 * line
    squared = sums[0:1, KRY : KRY + 1] + jnp.sum(quadratic, axis=1, keepdims=True)
    norm = jnp.sqrt(jnp.maximum(squared, 0.0) + 1e-06)
    next_ref[...] = remain / norm
    hess = jnp.where(lane == KRY, norm, sums[0:1])
    hess_ref[...] = hess[0, : KRY + 1]


def reduce_groups(segs):
    def number(place, inner):
        seg, y = place
        return seg * PEN + 16 * y + inner

    places = [(seg, y) for seg in range(segs) for y in range(2)]
    columns = [[number(place, inner) for inner in range(16)] for place in places]
    planes = [[number(place, inner) for place in places] for inner in range(16)]
    return columns, planes


def body(state, krylov):
    pen = lax.axis_index("pen")
    segs = lax.axis_size("seg")
    numbers = np.arange(NX)
    signed = np.where(numbers <= NX // 2, numbers, numbers - NX).astype(np.float32)
    steps = np.arange(WIDE)
    rows = CUT * (16 * (pen // 16) + pen % 4) + (4 * CUT * (steps // CUT) + steps % CUT)
    mode = jnp.where(rows <= NZ // 2, rows, rows - NZ).astype(jnp.float32)
    ksquare = mode[:, None] ** 2 + signed[None, :] ** 2
    inverse = jnp.where(ksquare > 0, 1.0 / jnp.where(ksquare > 0, ksquare, 1.0), 0.0)
    damping = 1.0 / (1.0 + time_step * viscosity * ksquare)
    table, cas_z, slope_z = [jnp.asarray(t) for t in tables()]
    state_f = state.transpose(1, 0, 2)
    kry_f = krylov.transpose(0, 2, 1, 3)
    exchange = functools.partial(
        lax.all_to_all, axis_name="pen", split_axis=0, concat_axis=0, tiled=True
    )
    everywhere = functools.partial(
        lax.all_to_all, axis_name=("seg", "pen"), split_axis=0, concat_axis=0, tiled=True
    )
    columns, planes = reduce_groups(segs)
    ring = [(s, (s + 1) % segs) for s in range(segs)]

    inputs = [state_f, kry_f]
    if not INTERPRET:
        inputs = [pltpu.with_memory_space_constraint(x, pltpu.HBM) for x in inputs]
    packed = pl.pallas_call(
        gather_rows,
        in_specs=[pl.BlockSpec(memory_space=pl.ANY)] * 2,
        out_specs=pl.BlockSpec(memory_space=pltpu.VMEM),
        scratch_shapes=[
            pltpu.VMEM((CUT, PLANES, NX), jnp.float32),
            pltpu.VMEM((CUT, PLANES, NX), jnp.float32),
            pltpu.SemaphoreType.DMA((2,)),
        ],
        out_shape=f32(4, 72, TILE),
        compiler_params=pltpu.CompilerParams(vmem_limit_bytes=24 << 20),
        interpret=INTERPRET,
    )(*inputs)
    packed = exchange(packed, axis_index_groups=PEERS)
    both = (f32(TEAM, 144, TILE), f32(2, WIDE, NX))
    send, fields = call(
        first_kernel, both, [packed, inverse, table], flops=700_000_000, moved=3_000_000
    )
    for repeat in range(STEPS):
        recv = exchange(send, axis_index_groups=TEAMS)
        modes = call(
            grid_kernel,
            f32(TEAM, WIDE, TILE),
            [recv, cas_z, slope_z],
            flops=900_000_000,
            moved=2_500_000,
        )
        recv = exchange(modes, axis_index_groups=TEAMS)
        if repeat < STEPS - 1:
            send, fields = call(
                middle_kernel,
                both,
                [recv, fields, damping, inverse, table],
                flops=900_000_000,
                moved=3_000_000,
            )
    ends = call(
        last_kernel,
        f32(4, 72, TILE),
        [recv, fields, damping, table],
        flops=200_000_000,
        moved=1_500_000,
    )
    ends = exchange(ends, axis_index_groups=PEERS)
    tangent = lax.ppermute(ends[:, 36:72].reshape(144, TILE), "seg", ring)
    gram = call(
        gram_kernel,
        f32(8, TILE),
        [kry_f],
        [pltpu.VMEM((KRY * KRY, TILE), jnp.float32)],
        flops=10_000_000,
        moved=1_300_000,
    )
    base, gram = lax.optimization_barrier((ends[:, 0:36].reshape(144, TILE), gram))
    base = lax.ppermute(base, "seg", ring)
    image, partial = call(
        dots_kernel,
        [f32(CUT, PLANES, NX), f32(16, 8, TILE)],
        [tangent, kry_f, gram],
        [pltpu.VMEM((TILE, TILE), jnp.float32)],
        flops=1_000_000,
        moved=1_300_000,
    )
    sums = everywhere(partial, axis_index_groups=columns)
    sums = jnp.sum(sums, axis=0)
    sums, base = lax.optimization_barrier((sums, base))
    sums = jnp.broadcast_to(sums[None], (2 * segs, 8, TILE))
    sums = everywhere(sums, axis_index_groups=planes)
    residual, vector, hess = call(
        finish_kernel,
        [f32(CUT, PLANES, NX)] * 2 + [f32(KRY + 1)],
        [sums, kry_f, image, state_f, base],
        flops=1_000_000,
        moved=1_500_000,
        keep=False,
    )
    return (residual.transpose(1, 0, 2), vector.transpose(1, 0, 2), hess)


def solution(mesh):
    return jax.shard_map(
        body,
        mesh=mesh,
        in_specs=(P("seg", "pen", None), P(None, "seg", "pen", None)),
        out_specs=(P("seg", "pen", None), P("seg", "pen", None), P()),
        check_vma=False,
    )
```

```python
import functools

import jax
import jax.numpy as jnp
import numpy as np
from jax import lax
from jax.experimental import pallas as pl
from jax.experimental.pallas import tpu as pltpu
from jax.sharding import PartitionSpec as P


NX = 384
NZ = 384
PLANES = 4
STEPS = 2
KRY = 16
SEGS = 16
PEN = 32
CUT = NZ // PEN
TEAM = 8
WIDE = NZ // TEAM
TILE = 128
INTERPRET = False

time_step = 0.0003
viscosity = 0.0226


def pen_index(y, team, member):
    return 16 * y + 4 * team + member


TEAMS = [[pen_index(y, q, r) for y in range(2) for r in range(4)] for q in range(4)]
PEERS = [[pen_index(y, q, r) for q in range(4)] for y in range(2) for r in range(4)]


def row_order():
    rows = []
    for y in range(2):
        for r in range(4):
            for q in range(4):
                rows += [CUT * pen_index(y, q, r) + n for n in range(CUT)]
    return np.array(rows)


def split_table(table):
    high = np.asarray(table, dtype=np.float32).astype(jnp.bfloat16)
    low = np.asarray(table - high.astype(np.float64), dtype=np.float32).astype(jnp.bfloat16)
    return np.concatenate([high, low], 0)


@functools.lru_cache(None)
def tables():
    count = NX
    k = np.arange(count)
    angle = 2.0 * np.pi * (np.outer(k, k) % count) / count
    cas = np.cos(angle) + np.sin(angle)
    signed = np.where(k <= count // 2, k, k - count)
    slopes = np.where(k == count // 2, 0, signed)
    slope = slopes[:, None] * (np.cos(angle) - np.sin(angle))
    order = row_order()
    pick = np.ix_(order, order)
    return (
        split_table(np.concatenate([cas, slope], 1)),
        split_table(cas[pick]),
        split_table(slope[pick].T),
    )


def halves(value):
    high = value.astype(jnp.bfloat16)
    low = (value - high.astype(jnp.float32)).astype(jnp.bfloat16)
    return high, low


def mm(a, b):
    return jnp.dot(a, b, preferred_element_type=jnp.float32)


def times_table(value, table_ref):
    high, low = halves(value)
    upper, lower = table_ref[0:NX, :], table_ref[NX : 2 * NX, :]
    left = jnp.concatenate([high, low, high], 1)
    return mm(left, jnp.concatenate([upper, upper, lower], 0))


def few_times_table(value, table_ref):
    high, low = halves(value)
    n = value.shape[0]
    both = mm(jnp.concatenate([high, low], 0), table_ref[0:NX, 0:NX])
    return both[0:n] + both[n : 2 * n] + mm(high, table_ref[NX : 2 * NX, 0:NX])


def table_times(table_ref, value):
    high, low = halves(value)
    upper, lower = table_ref[0:NX, :], table_ref[NX : 2 * NX, :]
    left = jnp.concatenate([upper, upper, lower], 1)
    return mm(left, jnp.concatenate([high, low, high], 0))


def call(kernel, outs, operands, scratch=(), flops=0, moved=0, keep=True):
    vmem = pl.BlockSpec(memory_space=pltpu.VMEM)
    single = not isinstance(outs, (list, tuple))
    shapes = [outs] if single else list(outs)
    if not INTERPRET:
        operands = [pltpu.with_memory_space_constraint(x, pltpu.VMEM) for x in operands]
        shapes = [pltpu.VMEM(x.shape, x.dtype) for x in shapes] if keep else shapes
    results = pl.pallas_call(
        kernel,
        in_specs=[vmem] * len(operands),
        out_specs=[vmem] * len(shapes),
        out_shape=shapes,
        scratch_shapes=list(scratch),
        cost_estimate=pl.CostEstimate(flops=flops, bytes_accessed=moved, transcendentals=0),
        compiler_params=pltpu.CompilerParams(vmem_limit_bytes=24 << 20),
        interpret=INTERPRET,
    )(*operands)
    return results[0] if single else results


def f32(*shape):
    return jax.ShapeDtypeStruct(shape, jnp.float32)


def tile(t):
    return slice(TILE * t, TILE * (t + 1))


def gather_rows(state_ref, last_ref, out_ref):
    for q in range(4):
        for member, ref in enumerate((state_ref, last_ref)):
            for t in range(3):
                row = 36 * member + CUT * t
                out_ref[q, row : row + CUT, :] = ref[:, q, tile(t)]


def spread(fields, inverse_ref, table_ref, send_ref):
    base, tangent = fields
    inverse = inverse_ref[...]
    spectra = jnp.concatenate([base * inverse, tangent * inverse, base, tangent], 0)
    both = times_table(spectra, table_ref)
    values, slopes = both[:, 0:NX], both[:, NX : 2 * NX]
    for m in range(TEAM):
        cut = slice(WIDE * m, WIDE * (m + 1))
        v = [values[WIDE * k : WIDE * (k + 1), cut] for k in range(4)]
        s = [slopes[WIDE * k : WIDE * (k + 1), cut] for k in range(4)]
        parts = [v[0], v[1], s[2][:, :32], v[2], v[3], s[2][:, 32:], s[3][:, :16]]
        block = jnp.concatenate(parts + [s[0], s[1], s[3][:, 16:]], 1)
        for t in range(3):
            send_ref[m, WIDE * t : WIDE * (t + 1), :] = block[:, tile(t)]


def first_kernel(recv_ref, inverse_ref, table_ref, send_ref, fields_ref):
    for q in range(4):
        for member in range(2):
            for t in range(3):
                row = 36 * member + CUT * t
                fields_ref[member, CUT * q : CUT * (q + 1), tile(t)] = recv_ref[
                    q, row : row + CUT, :
                ]
    spread((fields_ref[0], fields_ref[1]), inverse_ref, table_ref, send_ref)


def grid_kernel(recv_ref, cas_ref, slope_ref, send_ref):
    tiles = [
        jnp.concatenate([recv_ref[m, WIDE * t : WIDE * (t + 1), :] for m in range(TEAM)], 0)
        for t in range(3)
    ]
    tiles.append(jnp.concatenate([x[:, 96:] for x in (tiles[0], tiles[1], tiles[2], tiles[0])], 1))
    along_z = table_times(slope_ref, jnp.concatenate(tiles[0:2], 1))
    along_x = table_times(cas_ref, jnp.concatenate(tiles[2:4], 1))
    psi_z, vort_z = along_z[:, tile(0)], along_z[:, tile(1)]
    psi_x, vort_x = along_x[:, tile(0)], along_x[:, tile(1)]
    base = lax.broadcasted_iota(jnp.int32, (NZ, TILE), 1) < WIDE

    def moved(x):
        return pltpu.roll(x, WIDE, 1)

    first = psi_x * jnp.where(base, vort_z, moved(vort_z))
    first = first - psi_z * jnp.where(base, vort_x, moved(vort_x))
    second = moved(psi_x) * vort_z - moved(psi_z) * vort_x
    total = first + jnp.where(base, 0.0, second)
    modes = table_times(cas_ref, total)
    for m in range(TEAM):
        send_ref[m] = modes[WIDE * m : WIDE * (m + 1), :]


def advanced(recv_ref, fields_ref, damping_ref, table_ref):
    lines = [
        jnp.concatenate(
            [recv_ref[m, :, WIDE * member : WIDE * (member + 1)] for m in range(TEAM)], 1
        )
        for member in range(2)
    ]
    forcing = few_times_table(jnp.concatenate(lines, 0), table_ref)
    scale = time_step / (NX * NZ)
    damping = damping_ref[...]
    return [
        (fields_ref[member] + scale * forcing[WIDE * member : WIDE * (member + 1)]) * damping
        for member in range(2)
    ]


def middle_kernel(
    recv_ref, old_ref, damping_ref, inverse_ref, table_ref, send_ref, fields_ref
):
    fields = advanced(recv_ref, old_ref, damping_ref, table_ref)
    fields_ref[0] = fields[0]
    fields_ref[1] = fields[1]
    spread(fields, inverse_ref, table_ref, send_ref)


def last_kernel(recv_ref, old_ref, damping_ref, table_ref, out_ref):
    fields = advanced(recv_ref, old_ref, damping_ref, table_ref)
    for member in range(2):
        for q in range(4):
            for t in range(3):
                row = 36 * member + CUT * t
                out_ref[q, row : row + CUT, :] = fields[member][
                    CUT * q : CUT * (q + 1), tile(t)
                ]


def row_sums(value):
    ones = jnp.ones((8, TILE), jnp.bfloat16)
    first = value.astype(jnp.bfloat16)
    rest = value - first.astype(jnp.float32)
    second = rest.astype(jnp.bfloat16)
    third = (rest - second.astype(jnp.float32)).astype(jnp.bfloat16)
    dims = (((1,), (1,)), ((), ()))
    total = jnp.zeros((8, value.shape[0]), jnp.float32)
    for part in (third, second, first):
        total = total + lax.dot_general(ones, part, dims, preferred_element_type=jnp.float32)
    return total


def fold(value):
    return jnp.sum(value, axis=0, keepdims=True)


def fold(value):
    line = value[:, tile(0)] + value[:, tile(1)] + value[:, tile(2)]
    return jnp.sum(line, axis=0, keepdims=True)


def gram_kernel(kry_ref, out_ref, keep):
    for a in range(0, KRY, 4):
        for b in range(0, a + 1, 4):

            def step(g, sums):
                left = [kry_ref[a + i, g] for i in range(4)]
                right = [kry_ref[b + j, g] for j in range(4)]
                pairs = [(i, j) for i in range(4) for j in range(4)]
                return tuple(sums[4 * i + j] + left[i] * right[j] for i, j in pairs)

            zero = jnp.zeros((PLANES, NX), jnp.float32)
            sums = lax.fori_loop(0, CUT, step, (zero,) * 16, unroll=3)
            for i in range(4):
                for j in range(4):
                    line = fold(sums[4 * i + j])
                    keep[KRY * (a + i) + b + j : KRY * (a + i) + b + j + 1, :] = line
                    if a != b:
                        keep[KRY * (b + j) + a + i : KRY * (b + j) + a + i + 1, :] = line
    packed = row_sums(keep[...])
    row = lax.broadcasted_iota(jnp.int32, (8, TILE), 0)
    out_ref[...] = jnp.where(
        row == 1, packed[:, 0:TILE], jnp.where(row == 2, packed[:, TILE : 2 * TILE], 0.0)
    )


def place(planes_ref, out_ref):
    for p in range(PLANES):
        for t in range(3):
            row = 36 * p + CUT * t
            out_ref[:, p, tile(t)] = planes_ref[row : row + CUT, :]


def dots_kernel(planes_ref, kry_ref, gram_ref, image_ref, out_ref, keep):
    place(planes_ref, image_ref)
    image = image_ref[...] - kry_ref[KRY - 1]
    image_ref[...] = image
    keep[...] = jnp.zeros_like(keep)
    for k in range(KRY):
        keep[k : k + 1, :] = fold(jnp.sum(kry_ref[k] * image, axis=0))
    keep[KRY : KRY + 1, :] = fold(jnp.sum(image * image, axis=0))
    packed = row_sums(keep[...])
    row = lax.broadcasted_iota(jnp.int32, (8, TILE), 0)
    sums = jnp.where(row == 0, packed, gram_ref[...])
    for m in range(out_ref.shape[0]):
        out_ref[m] = sums


def finish_kernel(
    sums_ref, kry_ref, image_ref, state_ref, planes_ref, residual_ref, next_ref, hess_ref
):
    place(planes_ref, residual_ref)
    residual_ref[...] = residual_ref[...] - state_ref[...]
    total = float(SEGS * PLANES * NZ * NX)
    sums = sums_ref[0]
    for s in range(1, sums_ref.shape[0]):
        sums = sums + sums_ref[s]
    sums = sums / total
    coeffs = [sums[0:1, k : k + 1] for k in range(KRY)]
    remain = image_ref[...]
    for k in range(KRY):
        remain = remain - coeffs[k] * kry_ref[k]
    lane = lax.broadcasted_iota(jnp.int32, (1, TILE), 1)
    inner = jnp.zeros((1, TILE), jnp.float32)
    outer = [inner, inner]
    for k in range(KRY):
        inner = jnp.where(lane % KRY == k, coeffs[k], inner)
        half, block = k // 8, k % 8
        outer[half] = jnp.where(lane // KRY == block, coeffs[k], outer[half])
    line = jnp.where(lane < KRY, sums[0:1] * sums[0:1], 0.0)
    quadratic = inner * (outer[0] * sums[1:2] + outer[1] * sums[2:3]) - 2.0 * line
    squared = sums[0:1, KRY : KRY + 1] + jnp.sum(quadratic, axis=1, keepdims=True)
    norm = jnp.sqrt(jnp.maximum(squared, 0.0) + 1e-06)
    next_ref[...] = remain / norm
    hess = jnp.where(lane == KRY, norm, sums[0:1])
    hess_ref[...] = hess[0, : KRY + 1]


def reduce_groups(segs):
    def number(place, inner):
        seg, y = place
        return seg * PEN + 16 * y + inner

    places = [(seg, y) for seg in range(segs) for y in range(2)]
    columns = [[number(place, inner) for inner in range(16)] for place in places]
    planes = [[number(place, inner) for place in places] for inner in range(16)]
    return columns, planes


def body(state, krylov):
    pen = lax.axis_index("pen")
    segs = lax.axis_size("seg")
    numbers = jnp.arange(NX)
    signed = jnp.where(numbers <= NX // 2, numbers, numbers - NX).astype(jnp.float32)
    steps = jnp.arange(WIDE)
    rows = CUT * (16 * (pen // 16) + pen % 4) + (4 * CUT * (steps // CUT) + steps % CUT)
    mode = jnp.where(rows <= NZ // 2, rows, rows - NZ).astype(jnp.float32)
    ksquare = mode[:, None] ** 2 + signed[None, :] ** 2
    inverse = jnp.where(ksquare > 0, 1.0 / jnp.where(ksquare > 0, ksquare, 1.0), 0.0)
    damping = 1.0 / (1.0 + time_step * viscosity * ksquare)
    table, cas_z, slope_z = [jnp.asarray(t) for t in tables()]
    state_f = state.transpose(1, 0, 2)
    kry_f = krylov.transpose(0, 2, 1, 3)
    exchange = functools.partial(
        lax.all_to_all, axis_name="pen", split_axis=0, concat_axis=0, tiled=True
    )
    everywhere = functools.partial(
        lax.all_to_all, axis_name=("seg", "pen"), split_axis=0, concat_axis=0, tiled=True
    )
    columns, planes = reduce_groups(segs)
    ring = [(s, (s + 1) % segs) for s in range(segs)]

    whole = pl.BlockSpec((CUT, PLANES, NX), lambda i: (0, 0, 0))
    last = pl.BlockSpec((None, CUT, PLANES, NX), lambda i: (KRY - 1, 0, 0, 0))
    inputs = [state_f, kry_f]
    if not INTERPRET:
        inputs = [pltpu.with_memory_space_constraint(x, pltpu.HBM) for x in inputs]
    packed = pl.pallas_call(
        gather_rows,
        grid=(1,),
        in_specs=[whole, last],
        out_specs=pl.BlockSpec((4, 72, TILE), lambda i: (0, 0, 0)),
        out_shape=f32(4, 72, TILE) if INTERPRET else pltpu.VMEM((4, 72, TILE), jnp.float32),
        compiler_params=pltpu.CompilerParams(vmem_limit_bytes=24 << 20),
        interpret=INTERPRET,
    )(*inputs)
    packed, inverse, damping = lax.optimization_barrier((packed, inverse, damping))
    packed = exchange(packed, axis_index_groups=PEERS)
    both = (f32(TEAM, 144, TILE), f32(2, WIDE, NX))
    send, fields = call(
        first_kernel, both, [packed, inverse, table], flops=700_000_000, moved=3_000_000
    )
    for repeat in range(STEPS):
        recv = exchange(send, axis_index_groups=TEAMS)
        modes = call(
            grid_kernel,
            f32(TEAM, WIDE, TILE),
            [recv, cas_z, slope_z],
            flops=900_000_000,
            moved=2_500_000,
        )
        recv = exchange(modes, axis_index_groups=TEAMS)
        if repeat < STEPS - 1:
            send, fields = call(
                middle_kernel,
                both,
                [recv, fields, damping, inverse, table],
                flops=900_000_000,
                moved=3_000_000,
            )
    ends = call(
        last_kernel,
        f32(4, 72, TILE),
        [recv, fields, damping, table],
        flops=200_000_000,
        moved=1_500_000,
    )
    ends = exchange(ends, axis_index_groups=PEERS)
    tangent = lax.ppermute(ends[:, 36:72].reshape(144, TILE), "seg", ring)
    gram = call(
        gram_kernel,
        f32(8, TILE),
        [kry_f],
        [pltpu.VMEM((KRY * KRY, TILE), jnp.float32)],
        flops=10_000_000,
        moved=1_300_000,
    )
    base, gram = lax.optimization_barrier((ends[:, 0:36].reshape(144, TILE), gram))
    base = lax.ppermute(base, "seg", ring)
    image, partial = call(
        dots_kernel,
        [f32(CUT, PLANES, NX), f32(16, 8, TILE)],
        [tangent, kry_f, gram],
        [pltpu.VMEM((TILE, TILE), jnp.float32)],
        flops=1_000_000,
        moved=1_300_000,
    )
    sums = everywhere(partial, axis_index_groups=columns)
    sums = jnp.sum(sums, axis=0)
    sums, base = lax.optimization_barrier((sums, base))
    sums = jnp.broadcast_to(sums[None], (2 * segs, 8, TILE))
    sums = everywhere(sums, axis_index_groups=planes)
    residual, vector, hess = call(
        finish_kernel,
        [f32(CUT, PLANES, NX)] * 2 + [f32(KRY + 1)],
        [sums, kry_f, image, state_f, base],
        flops=1_000_000,
        moved=1_500_000,
        keep=False,
    )
    return (residual.transpose(1, 0, 2), vector.transpose(1, 0, 2), hess)


def solution(mesh):
    return jax.shard_map(
        body,
        mesh=mesh,
        in_specs=(P("seg", "pen", None), P(None, "seg", "pen", None)),
        out_specs=(P("seg", "pen", None), P("seg", "pen", None), P()),
        check_vma=False,
    )
```
